256 devices in a mesh: prow: 32 (over z, y), pcol: 8 (over x, core).
Axes of the slice: x: 4, y: 4, z: 8, core: 2. Of those that a mesh axis runs over, the one named last changes fastest.
Arguments:
- right_side: bfloat16 [3, 32, 256, 128], P(None, 'prow'), may hold values from -6 to 6
- lower_blocks: bfloat16 [3, 32, 256, 8192], P(None, 'prow', None, 'pcol'), may hold values from -0.0625 to 0.0625
- upper_blocks: bfloat16 [3, 32, 256, 8192], P(None, 'prow', None, 'pcol'), may hold values from -0.0625 to 0.0625
- lower_inverse: bfloat16 [3, 32, 256, 256], P(None, 'prow'), as said below
- upper_inverse: bfloat16 [3, 32, 256, 256], P(None, 'prow'), as said below
- pattern: int32 [3, 32, 32], replicated, may hold values 0 or 1
Outputs:
- solution: bfloat16 [3, 32, 256, 128], P(None, 'prow')
The draws below stay inside these ranges and needn't reach their ends.
Inputs may be any that keep to these rules, and one draw needn't show every extreme that they name: `lower_inverse`: each block is lower triangular with its diagonal between 0.6 and 1.4. `upper_inverse`: each block is upper triangular with its diagonal between 0.6 and 1.4.
All inputs are finite; a program needn't handle non-finite values.
Results may differ from the reference program's by a relative error of at most 0.007.
Values may be sent and summed in bfloat16 or wider, within the bound.
A program may use at most 64 MiB of HBM per device.

```python
import math
import jax
import jax.numpy as jnp
from jax import lax

B = 256
LEV = 3
NR = 32
PAIRS = 3
W = 128


def triangle_blocks(key, upper_side):
    first_key, second_key = jax.random.split(key)
    diagonal = jax.random.uniform(first_key, (LEV, NR, B), jnp.float32, 0.6, 1.4)
    offside = jax.random.normal(second_key, (LEV, NR, B, B), jnp.float32) * (0.8 / math.sqrt(B))
    row_ids = jnp.arange(B)[:, None]
    col_ids = jnp.arange(B)[None, :]
    if upper_side:
        keep_mask = col_ids > row_ids
    else:
        keep_mask = col_ids < row_ids
    identity = (row_ids == col_ids).astype(jnp.float32)
    matrix = jnp.where(keep_mask, offside, 0.0) + identity * diagonal[..., None]
    return matrix.astype(jnp.bfloat16)


def draw_lower_inverse(key, part):
    return triangle_blocks(jax.random.fold_in(key, 11), False)


def draw_upper_inverse(key, part):
    return triangle_blocks(jax.random.fold_in(key, 23), True)


def set_ends(array, stream_key, least, top_value):
    longest = array.shape.index(max(array.shape))
    spots = []
    for shift in (0, 1):
        where = [jax.random.randint(jax.random.fold_in(stream_key, axis), (), 0, length) for axis, length in enumerate(array.shape)]
        where[longest] = (where[longest] + shift) % array.shape[longest]
        spots.append(tuple(where))
    return array.at[spots[0]].set(least).at[spots[1]].set(top_value)


def steps_of(key, shape, cuts, low, high):
    factor_of = 1.0
    for dim, shards_of in cuts:
        heights = jax.random.uniform(jax.random.fold_in(jax.random.fold_in(key, 6), dim), (shards_of,), jnp.float32, low / len(cuts), high / len(cuts))
        factor_of = factor_of * jnp.repeat(jnp.exp(heights), shape[dim] // shards_of).reshape((-1,) + (1,) * (len(shape) - 1 - dim))
    return factor_of


def gaussian(own_key, extent, scale, reach, pieces=(), kind=jnp.bfloat16):
    values = scale * jax.random.normal(own_key, extent, jnp.float32)
    if pieces:
        values = values * steps_of(own_key, extent, pieces, -0.22, 0.18)
    return jnp.clip(values, -reach, reach).astype(kind)


def setup_inputs(seed: int = 0) -> dict:
    arg_keys = jax.random.split(jax.random.key(seed), 7)
    right_side = gaussian(arg_keys[0], (LEV, NR, B, W), 1.0, 6.0, ((1, 32),))
    lower_blocks = gaussian(arg_keys[1], (PAIRS, NR, B, NR * B), ((LEV - 1) * NR * B // 2) ** -0.5, 0.0625, ((1, 32), (3, 8)))
    upper_blocks = gaussian(arg_keys[2], (PAIRS, NR, B, NR * B), ((LEV - 1) * NR * B // 2) ** -0.5, 0.0625, ((1, 32), (3, 8)))
    lower_inverse = draw_lower_inverse(jax.random.fold_in(arg_keys[6], 71), 0)
    upper_inverse = draw_upper_inverse(jax.random.fold_in(arg_keys[6], 71), 0)
    pattern = set_ends((jax.random.randint(arg_keys[5], (PAIRS, NR, NR), 0, 2) < 1).astype(jnp.int32), jax.random.fold_in(arg_keys[5], 1), 0, 1)
    return {"right_side": right_side, "lower_blocks": lower_blocks, "upper_blocks": upper_blocks, "lower_inverse": lower_inverse, "upper_inverse": upper_inverse, "pattern": pattern}


def pair_index(later, earlier):
    return later * (later - 1) // 2 + earlier


def masked_matrix(blocks, keep_mask):
    expanded = jnp.repeat(jnp.repeat(keep_mask > 0, B, axis=0), B, axis=1)
    flat = blocks.reshape(NR * B, NR * B)
    return jnp.where(expanded, flat, jnp.zeros((), flat.dtype))


def apply_inverse(inverse, values):
    return jnp.einsum("rij,rjw->riw", inverse.astype(jnp.float32), values, precision=lax.Precision.HIGHEST)


def reference(right_side, lower_blocks, upper_blocks, lower_inverse, upper_inverse, pattern):
    solved = []
    for level_now in range(LEV):
        summed = jnp.zeros((NR * B, W), jnp.float32)
        for earlier in range(level_now):
            pair_now = pair_index(level_now, earlier)
            matrix = masked_matrix(lower_blocks[pair_now], pattern[pair_now])
            summed = summed + jnp.dot(matrix, solved[earlier].reshape(NR * B, W), preferred_element_type=jnp.float32)
        values = right_side[level_now].astype(jnp.float32) - summed.reshape(NR, B, W)
        solved.append(apply_inverse(lower_inverse[level_now], values).astype(jnp.bfloat16))
    results = [None] * LEV
    for level_now in reversed(range(LEV)):
        summed = jnp.zeros((NR * B, W), jnp.float32)
        for later in range(level_now + 1, LEV):
            pair_now = pair_index(later, level_now)
            matrix = masked_matrix(upper_blocks[pair_now], pattern[pair_now].T)
            summed = summed + jnp.dot(matrix, results[later].reshape(NR * B, W), preferred_element_type=jnp.float32)
        values = solved[level_now].astype(jnp.float32) - summed.reshape(NR, B, W)
        results[level_now] = apply_inverse(upper_inverse[level_now], values).astype(jnp.bfloat16)
    return jnp.stack(results)
```

```python
import functools

import jax
import jax.numpy as jnp
from jax import lax
from jax.experimental import pallas as pl
from jax.experimental.pallas import tpu as pltpu
from jax.sharding import PartitionSpec as P

MESH = pl.DeviceIdType.MESH
F32 = jnp.float32
BF16 = jnp.bfloat16


def mm(a, b):
    return jnp.dot(a, b, preferred_element_type=F32)


def kernel(
    n_rows, n_cols, n_group,
    rhs_hbm, low_hbm, upp_hbm, linv_hbm, uinv_hbm, pat_hbm,
    out_hbm,
    rhs, low, upp, linv, uinv, pat,
    first, base1, base2, base0, carry, prod, land, slices, fetched, padded, n_hi, n_lo,
    load_sem, pat_sem, cast_send, cast_recv, sum_send, sum_recv, out_send, out_recv,
):
    size = rhs.shape[1]
    part = size // n_cols
    row = lax.axis_index("prow")
    col = lax.axis_index("pcol")
    owner_col = row // n_group
    place = row % n_group
    n_outer = n_rows // n_group

    barrier = pltpu.get_barrier_semaphore()

    def target_row(step):
        i, j = step // n_group, step % n_group
        d_outer = n_outer // 2 + ((i + 1) // 2) * (1 - 2 * (i % 2))
        d_inner = n_group // 2 + ((j + 1) // 2) * (1 - 2 * (j % 2))
        outer = (row // n_group + d_outer) % n_outer
        inner = (row % n_group + d_inner) % n_group
        return outer * n_group + inner

    is_own = owner_col == col

    for q in range(n_cols):
        for b in range(n_group):
            src_row = col * n_group + b
            if True:
                other = jnp.logical_or(src_row != row, q != col)

                @pl.when(other)
                def _():
                    pl.semaphore_signal(barrier, inc=1, device_id=(src_row, q), device_id_type=MESH)

        @pl.when(q != col)
        def _():
            pl.semaphore_signal(barrier, inc=1, device_id=(row, q), device_id_type=MESH)

    loads = [
        pltpu.make_async_copy(linv_hbm.at[:, 0], linv, load_sem.at[0]),
        pltpu.make_async_copy(rhs_hbm.at[:, 0], rhs, load_sem.at[1]),
        pltpu.make_async_copy(pat_hbm, pat, pat_sem),
        pltpu.make_async_copy(low_hbm.at[0, 0], low.at[0], load_sem.at[2]),
        pltpu.make_async_copy(uinv_hbm.at[:, 0], uinv, load_sem.at[3]),
        pltpu.make_async_copy(low_hbm.at[1, 0], low.at[1], load_sem.at[4]),
        pltpu.make_async_copy(low_hbm.at[2, 0], low.at[2], load_sem.at[5]),
        pltpu.make_async_copy(upp_hbm.at[:, 0], upp, load_sem.at[6]),
    ]
    for copy in loads:
        copy.start()

    own_rows = pl.ds(pl.multiple_of(col * part, part), part)

    def cast_copy(rnd, step):
        source = first.at[own_rows] if rnd == 0 else slices.at[rnd]
        where = pl.ds(pl.multiple_of(place * size + col * part, part), part)
        return pltpu.make_async_remote_copy(
            src_ref=source,
            dst_ref=fetched.at[rnd, where],
            send_sem=cast_send.at[rnd],
            recv_sem=cast_recv.at[rnd],
            device_id=(target_row(step), owner_col),
            device_id_type=MESH,
        )

    def cast_local(rnd):
        source = first.at[own_rows] if rnd == 0 else slices.at[rnd]
        where = pl.ds(pl.multiple_of(place * size + col * part, part), part)
        return pltpu.make_async_copy(source, fetched.at[rnd, where], cast_recv.at[rnd])

    def cast_start(rnd):
        def one(step, unused):
            cast_copy(rnd, step).start()
            return unused

        lax.fori_loop(0, n_rows - 1, one, 0)

        @pl.when(jnp.logical_not(is_own))
        def _():
            cast_copy(rnd, n_rows - 1).start()

        @pl.when(is_own)
        def _():
            cast_local(rnd).start()

    def cast_wait(rnd):
        pltpu.make_async_copy(fetched.at[rnd], fetched.at[rnd], cast_recv.at[rnd]).wait()

    def cast_drain(rnd):
        def one(step, unused):
            cast_copy(rnd, step).wait_send()
            return unused

        lax.fori_loop(0, n_rows - 1, one, 0)

        @pl.when(jnp.logical_not(is_own))
        def _():
            cast_copy(rnd, n_rows - 1).wait_send()

    def peer(step):
        return lax.rem(col + step, n_cols)

    def sum_copy(rnd, step):
        q = peer(step)
        return pltpu.make_async_remote_copy(
            src_ref=prod.at[rnd, pl.ds(pl.multiple_of(q * part, part), part)],
            dst_ref=land.at[rnd, col],
            send_sem=sum_send.at[rnd],
            recv_sem=sum_recv.at[rnd],
            device_id=(row, q),
            device_id_type=MESH,
        )

    order = [4, 3, 5, 2, 6, 1, 7]

    def scatter(rnd, value):
        prod[rnd] = value
        for step in order:
            sum_copy(rnd, step).start()
        land[rnd, col] = prod[rnd, own_rows]

    def summed(rnd):
        pltpu.make_async_copy(
            land.at[rnd, pl.ds(0, n_cols - 1)], land.at[rnd, pl.ds(0, n_cols - 1)], sum_recv.at[rnd]
        ).wait()
        total = land[rnd, 0]
        for q in range(1, n_cols):
            total = total + land[rnd, q]
        return total

    def out_copy(rnd, level, step):
        return pltpu.make_async_remote_copy(
            src_ref=slices.at[rnd],
            dst_ref=out_hbm.at[level, 0, own_rows],
            send_sem=out_send.at[level],
            recv_sem=out_recv.at[level],
            device_id=(row, peer(step)),
            device_id_type=MESH,
        )

    def share(rnd, level):
        for step in order:
            out_copy(rnd, level, step).start()
        pltpu.make_async_copy(slices.at[rnd], out_hbm.at[level, 0, own_rows], out_recv.at[level]).start()

    def share_wait(rnd, level):
        pltpu.make_async_copy(out_hbm.at[level, 0], out_hbm.at[level, 0], out_recv.at[level]).wait()
        for step in order:
            out_copy(rnd, level, step).wait_send()

    def fold_lower(pair, products):
        for b in range(n_group):
            cols = slice(b * size, (b + 1) * size)
            keep = pat[pair, row, col * n_group + b].astype(F32)
            low[pair, :, cols] = (products(low[pair, :, cols]) * keep).astype(BF16)

    def fold_upper(pair, level):
        for b in range(n_group):
            cols = slice(b * size, (b + 1) * size)
            keep = pat[pair, col * n_group + b, row].astype(F32)
            upp[pair, :, cols] = (mm(uinv[level], upp[pair, :, cols]) * keep).astype(BF16)

    loads[0].wait()
    loads[1].wait()
    first[...] = mm(linv[0], rhs[0]).astype(BF16)

    pl.semaphore_wait(barrier, n_rows + n_cols - 1 - is_own.astype(jnp.int32))
    cast_start(0)

    loads[2].wait()
    loads[3].wait()
    fold_lower(0, lambda block: mm(linv[1], block))
    base1[...] = mm(linv[1], rhs[1])
    loads[4].wait()
    both = mm(uinv[2], linv[2])
    n_hi[...] = both.astype(BF16)
    n_lo[...] = (both - n_hi[...].astype(F32)).astype(BF16)

    def through(block):
        return mm(n_hi[...], block) + mm(n_lo[...], block)

    base2[...] = through(rhs[2])
    base0[...] = mm(uinv[0], first[...])
    loads[5].wait()
    fold_lower(1, through)
    loads[6].wait()
    fold_lower(2, through)

    cast_wait(0)
    scatter(0, mm(low[0], fetched[0]))
    carry[...] = mm(low[1], fetched[0])
    slices[1] = (base1[own_rows] - summed(0)).astype(BF16)
    cast_start(1)

    loads[7].wait()
    fold_upper(2, 1)
    fold_upper(1, 0)
    fold_upper(0, 0)
    padded[...] = jnp.zeros_like(padded)
    padded[own_rows] = slices[1]

    cast_wait(1)
    scatter(1, carry[...] + mm(low[2], fetched[1]))
    carry[...] = mm(uinv[1], padded[...])
    slices[2] = (base2[own_rows] - summed(1)).astype(BF16)
    cast_start(2)
    share(2, 2)

    cast_wait(2)
    scatter(2, mm(upp[2], fetched[2]) - carry[...])
    carry[...] = mm(upp[1], fetched[2])
    slices[3] = (-summed(2)).astype(BF16)
    cast_start(3)
    share(3, 1)

    cast_wait(3)
    scatter(3, carry[...] + mm(upp[0], fetched[3]))
    slices[4] = (base0[own_rows] - summed(3)).astype(BF16)
    share(4, 0)

    for rnd in range(4):
        cast_drain(rnd)
        for step in order:
            sum_copy(rnd, step).wait_send()
    share_wait(2, 2)
    share_wait(3, 1)
    share_wait(4, 0)


def solution(mesh):
    n_rows, n_cols = mesh.shape["prow"], mesh.shape["pcol"]

    def body(right_side, lower_blocks, upper_blocks, lower_inverse, upper_inverse, pattern):
        levels, _, size, width = right_side.shape
        pairs, _, _, span = lower_blocks.shape
        n_group = span // size
        part = size // n_cols
        any_spec = pl.BlockSpec(memory_space=pl.ANY)
        return pl.pallas_call(
            functools.partial(kernel, n_rows, n_cols, n_group),
            out_shape=jax.ShapeDtypeStruct((levels, 1, size, width), BF16),
            in_specs=[any_spec] * 6,
            out_specs=any_spec,
            scratch_shapes=[
                pltpu.VMEM((levels, size, width), BF16),
                pltpu.VMEM((pairs, size, span), BF16),
                pltpu.VMEM((pairs, size, span), BF16),
                pltpu.VMEM((levels, size, size), BF16),
                pltpu.VMEM((levels, size, size), BF16),
                pltpu.SMEM(pattern.shape, jnp.int32),
                pltpu.VMEM((size, width), BF16),
                pltpu.VMEM((size, width), F32),
                pltpu.VMEM((size, width), F32),
                pltpu.VMEM((size, width), F32),
                pltpu.VMEM((size, width), F32),
                pltpu.VMEM((4, size, width), F32),
                pltpu.VMEM((4, n_cols, part, width), F32),
                pltpu.VMEM((5, part, width), BF16),
                pltpu.VMEM((4, span, width), BF16),
                pltpu.VMEM((size, width), BF16),
                pltpu.VMEM((size, size), BF16),
                pltpu.VMEM((size, size), BF16),
                pltpu.SemaphoreType.DMA((7,)),
                pltpu.SemaphoreType.DMA(()),
                pltpu.SemaphoreType.DMA((4,)),
                pltpu.SemaphoreType.DMA((4,)),
                pltpu.SemaphoreType.DMA((4,)),
                pltpu.SemaphoreType.DMA((4,)),
                pltpu.SemaphoreType.DMA((3,)),
                pltpu.SemaphoreType.DMA((3,)),
            ],
            compiler_params=pltpu.CompilerParams(collective_id=0, has_side_effects=True),
        )(right_side, lower_blocks, upper_blocks, lower_inverse, upper_inverse, pattern)

    placed = (
        P(None, "prow", None, None),
        P(None, "prow", None, "pcol"),
        P(None, "prow", None, "pcol"),
        P(None, "prow", None, None),
        P(None, "prow", None, None),
        P(),
    )
    return jax.shard_map(
        body, mesh=mesh, in_specs=placed, out_specs=P(None, "prow", None, None), check_vma=False
    )
```

```python
import functools

import jax
import jax.numpy as jnp
from jax import lax
from jax.experimental import pallas as pl
from jax.experimental.pallas import tpu as pltpu
from jax.sharding import PartitionSpec as P

MESH = pl.DeviceIdType.MESH
F32 = jnp.float32
BF16 = jnp.bfloat16


def mm(a, b):
    return jnp.dot(a, b, preferred_element_type=F32)


def kernel(
    n_rows, n_cols, n_group,
    rhs_hbm, low_hbm, upp_hbm, linv_hbm, uinv_hbm, pat_hbm,
    out_hbm,
    rhs, low, upp, linv, uinv, pat,
    first, base1, base2, base0, carry, prod, land, slices, fetched, padded, n_hi, n_lo,
    load_sem, pat_sem, cast_send, cast_recv, sum_send, sum_recv, out_send, out_recv,
):
    size = rhs.shape[1]
    part = size // n_cols
    row = lax.axis_index("prow")
    col = lax.axis_index("pcol")
    owner_col = row // n_group
    place = row % n_group
    n_outer = n_rows // n_group

    barrier = pltpu.get_barrier_semaphore()

    def target_row(step):
        i, j = step // n_group, step % n_group
        d_outer = n_outer // 2 + ((i + 1) // 2) * (1 - 2 * (i % 2))
        d_inner = n_group // 2 + ((j + 1) // 2) * (1 - 2 * (j % 2))
        outer = (row // n_group + d_outer) % n_outer
        inner = (row % n_group + d_inner) % n_group
        return outer * n_group + inner

    is_own = owner_col == col

    for q in range(n_cols):
        for b in range(n_group):
            src_row = col * n_group + b
            if True:
                other = jnp.logical_or(src_row != row, q != col)

                @pl.when(other)
                def _():
                    pl.semaphore_signal(barrier, inc=1, device_id=(src_row, q), device_id_type=MESH)

        @pl.when(q != col)
        def _():
            pl.semaphore_signal(barrier, inc=1, device_id=(row, q), device_id_type=MESH)

    loads = [
        pltpu.make_async_copy(linv_hbm.at[:, 0], linv, load_sem.at[0]),
        pltpu.make_async_copy(rhs_hbm.at[:, 0], rhs, load_sem.at[1]),
        pltpu.make_async_copy(pat_hbm, pat, pat_sem),
        pltpu.make_async_copy(low_hbm.at[0, 0], low.at[0], load_sem.at[2]),
        pltpu.make_async_copy(uinv_hbm.at[:, 0], uinv, load_sem.at[3]),
        pltpu.make_async_copy(low_hbm.at[1, 0], low.at[1], load_sem.at[4]),
        pltpu.make_async_copy(low_hbm.at[2, 0], low.at[2], load_sem.at[5]),
        pltpu.make_async_copy(upp_hbm.at[:, 0], upp, load_sem.at[6]),
    ]
    for copy in loads:
        copy.start()

    own_rows = pl.ds(pl.multiple_of(col * part, part), part)

    def cast_copy(rnd, step):
        source = first.at[own_rows] if rnd == 0 else slices.at[rnd]
        where = pl.ds(pl.multiple_of(place * size + col * part, part), part)
        return pltpu.make_async_remote_copy(
            src_ref=source,
            dst_ref=fetched.at[rnd, where],
            send_sem=cast_send.at[rnd],
            recv_sem=cast_recv.at[rnd],
            device_id=(target_row(step), owner_col),
            device_id_type=MESH,
        )

    def cast_local(rnd):
        source = first.at[own_rows] if rnd == 0 else slices.at[rnd]
        where = pl.ds(pl.multiple_of(place * size + col * part, part), part)
        return pltpu.make_async_copy(source, fetched.at[rnd, where], cast_recv.at[rnd])

    def cast_start(rnd):
        def one(step, unused):
            cast_copy(rnd, step).start()
            return unused

        lax.fori_loop(0, n_rows - 1, one, 0)

        @pl.when(jnp.logical_not(is_own))
        def _():
            cast_copy(rnd, n_rows - 1).start()

        @pl.when(is_own)
        def _():
            cast_local(rnd).start()

    def cast_wait(rnd):
        pltpu.make_async_copy(fetched.at[rnd], fetched.at[rnd], cast_recv.at[rnd]).wait()

    def cast_drain(rnd):
        def one(step, unused):
            cast_copy(rnd, step).wait_send()
            return unused

        lax.fori_loop(0, n_rows - 1, one, 0)

        @pl.when(jnp.logical_not(is_own))
        def _():
            cast_copy(rnd, n_rows - 1).wait_send()

    def peer(step):
        return lax.rem(col + step, n_cols)

    def sum_copy(rnd, step):
        q = peer(step)
        return pltpu.make_async_remote_copy(
            src_ref=prod.at[rnd, pl.ds(pl.multiple_of(q * part, part), part)],
            dst_ref=land.at[rnd, col],
            send_sem=sum_send.at[rnd],
            recv_sem=sum_recv.at[rnd],
            device_id=(row, q),
            device_id_type=MESH,
        )

    order = [4, 3, 5, 2, 6, 1, 7]

    def scatter(rnd, value):
        prod[rnd] = value.astype(BF16)
        for step in order:
            sum_copy(rnd, step).start()
        land[rnd, col] = prod[rnd, own_rows]

    def summed(rnd):
        pltpu.make_async_copy(
            land.at[rnd, pl.ds(0, n_cols - 1)], land.at[rnd, pl.ds(0, n_cols - 1)], sum_recv.at[rnd]
        ).wait()
        total = land[rnd, 0].astype(F32)
        for q in range(1, n_cols):
            total = total + land[rnd, q].astype(F32)
        return total

    def out_copy(rnd, level, step):
        return pltpu.make_async_remote_copy(
            src_ref=slices.at[rnd],
            dst_ref=out_hbm.at[level, 0, own_rows],
            send_sem=out_send.at[level],
            recv_sem=out_recv.at[level],
            device_id=(row, peer(step)),
            device_id_type=MESH,
        )

    def share(rnd, level):
        for step in order:
            out_copy(rnd, level, step).start()
        pltpu.make_async_copy(slices.at[rnd], out_hbm.at[level, 0, own_rows], out_recv.at[level]).start()

    def share_wait(rnd, level):
        pltpu.make_async_copy(out_hbm.at[level, 0], out_hbm.at[level, 0], out_recv.at[level]).wait()
        for step in order:
            out_copy(rnd, level, step).wait_send()

    def fold_lower(pair, products):
        for b in range(n_group):
            cols = slice(b * size, (b + 1) * size)
            keep = pat[pair, row, col * n_group + b].astype(F32)
            low[pair, :, cols] = (products(low[pair, :, cols]) * keep).astype(BF16)

    def fold_upper(pair, level):
        for b in range(n_group):
            cols = slice(b * size, (b + 1) * size)
            keep = pat[pair, col * n_group + b, row].astype(F32)
            upp[pair, :, cols] = (mm(uinv[level], upp[pair, :, cols]) * keep).astype(BF16)

    loads[0].wait()
    loads[1].wait()
    first[...] = mm(linv[0], rhs[0]).astype(BF16)

    pl.semaphore_wait(barrier, n_rows + n_cols - 1 - is_own.astype(jnp.int32))
    cast_start(0)

    loads[2].wait()
    loads[3].wait()
    fold_lower(0, lambda block: mm(linv[1], block))
    base1[...] = mm(linv[1], rhs[1])
    loads[4].wait()
    both = mm(uinv[2], linv[2])
    n_hi[...] = both.astype(BF16)
    n_lo[...] = (both - n_hi[...].astype(F32)).astype(BF16)

    def through(block):
        return mm(n_hi[...], block) + mm(n_lo[...], block)

    base2[...] = through(rhs[2])
    base0[...] = mm(uinv[0], first[...])
    loads[5].wait()
    fold_lower(1, through)
    loads[6].wait()
    fold_lower(2, through)

    cast_wait(0)
    scatter(0, mm(low[0], fetched[0]))
    carry[...] = mm(low[1], fetched[0])
    slices[1] = (base1[own_rows] - summed(0)).astype(BF16)
    cast_start(1)

    loads[7].wait()
    fold_upper(2, 1)
    fold_upper(1, 0)
    fold_upper(0, 0)
    padded[...] = jnp.zeros_like(padded)
    padded[own_rows] = slices[1]

    cast_wait(1)
    scatter(1, carry[...] + mm(low[2], fetched[1]))
    carry[...] = mm(uinv[1], padded[...])
    slices[2] = (base2[own_rows] - summed(1)).astype(BF16)
    cast_start(2)
    share(2, 2)

    cast_wait(2)
    scatter(2, mm(upp[2], fetched[2]) - carry[...])
    carry[...] = mm(upp[1], fetched[2])
    slices[3] = (-summed(2)).astype(BF16)
    cast_start(3)
    share(3, 1)

    cast_wait(3)
    scatter(3, carry[...] + mm(upp[0], fetched[3]))
    slices[4] = (base0[own_rows] - summed(3)).astype(BF16)
    share(4, 0)

    for rnd in range(4):
        cast_drain(rnd)
        for step in order:
            sum_copy(rnd, step).wait_send()
    share_wait(2, 2)
    share_wait(3, 1)
    share_wait(4, 0)


def solution(mesh):
    n_rows, n_cols = mesh.shape["prow"], mesh.shape["pcol"]

    def body(right_side, lower_blocks, upper_blocks, lower_inverse, upper_inverse, pattern):
        levels, _, size, width = right_side.shape
        pairs, _, _, span = lower_blocks.shape
        n_group = span // size
        part = size // n_cols
        any_spec = pl.BlockSpec(memory_space=pl.ANY)
        return pl.pallas_call(
            functools.partial(kernel, n_rows, n_cols, n_group),
            out_shape=jax.ShapeDtypeStruct((levels, 1, size, width), BF16),
            in_specs=[pl.BlockSpec(memory_space=pltpu.HBM)] * 6,
            out_specs=any_spec,
            scratch_shapes=[
                pltpu.VMEM((levels, size, width), BF16),
                pltpu.VMEM((pairs, size, span), BF16),
                pltpu.VMEM((pairs, size, span), BF16),
                pltpu.VMEM((levels, size, size), BF16),
                pltpu.VMEM((levels, size, size), BF16),
                pltpu.SMEM(pattern.shape, jnp.int32),
                pltpu.VMEM((size, width), BF16),
                pltpu.VMEM((size, width), F32),
                pltpu.VMEM((size, width), F32),
                pltpu.VMEM((size, width), F32),
                pltpu.VMEM((size, width), F32),
                pltpu.VMEM((4, size, width), BF16),
                pltpu.VMEM((4, n_cols, part, width), BF16),
                pltpu.VMEM((5, part, width), BF16),
                pltpu.VMEM((4, span, width), BF16),
                pltpu.VMEM((size, width), BF16),
                pltpu.VMEM((size, size), BF16),
                pltpu.VMEM((size, size), BF16),
                pltpu.SemaphoreType.DMA((7,)),
                pltpu.SemaphoreType.DMA(()),
                pltpu.SemaphoreType.DMA((4,)),
                pltpu.SemaphoreType.DMA((4,)),
                pltpu.SemaphoreType.DMA((4,)),
                pltpu.SemaphoreType.DMA((4,)),
                pltpu.SemaphoreType.DMA((3,)),
                pltpu.SemaphoreType.DMA((3,)),
            ],
            compiler_params=pltpu.CompilerParams(collective_id=0, has_side_effects=True, vmem_limit_bytes=24 * 1024 * 1024),
        )(*[pltpu.with_memory_space_constraint(x, pltpu.HBM) for x in (right_side, lower_blocks, upper_blocks, lower_inverse, upper_inverse, pattern)])

    placed = (
        P(None, "prow", None, None),
        P(None, "prow", None, "pcol"),
        P(None, "prow", None, "pcol"),
        P(None, "prow", None, None),
        P(None, "prow", None, None),
        P(),
    )
    return jax.shard_map(
        body, mesh=mesh, in_specs=placed, out_specs=P(None, "prow", None, None), check_vma=False
    )
```

```python
import functools

import jax
import jax.numpy as jnp
from jax import lax
from jax.experimental import pallas as pl
from jax.experimental.pallas import tpu as pltpu
from jax.sharding import PartitionSpec as P

MESH = pl.DeviceIdType.MESH
F32 = jnp.float32
BF16 = jnp.bfloat16


def mm(a, b):
    return jnp.dot(a, b, preferred_element_type=F32)


def kernel(
    n_rows, n_cols, n_group,
    rhs_hbm, low_hbm, upp_hbm, linv_hbm, uinv_hbm, pat_hbm,
    out_hbm,
    rhs, low, upp, linv, uinv, pat,
    first, base1, base2, base0, carry, prod, land, slices, fetched, padded, n_hi, n_lo,
    load_sem, pat_sem, cast_send, cast_recv, sum_send, sum_recv, out_send, out_recv,
):
    size = rhs.shape[1]
    part = size // n_cols
    row = lax.axis_index("prow")
    col = lax.axis_index("pcol")
    owner_col = row // n_group
    place = row % n_group
    n_outer = n_rows // n_group

    barrier = pltpu.get_barrier_semaphore()

    def target_row(step):
        i, j = step // n_group, step % n_group
        d_outer = n_outer // 2 + ((i + 1) // 2) * (1 - 2 * (i % 2))
        d_inner = n_group // 2 + ((j + 1) // 2) * (1 - 2 * (j % 2))
        outer = (row // n_group + d_outer) % n_outer
        inner = (row % n_group + d_inner) % n_group
        return outer * n_group + inner

    is_own = owner_col == col

    for q in range(n_cols):
        for b in range(n_group):
            src_row = col * n_group + b
            if True:
                other = jnp.logical_or(src_row != row, q != col)

                @pl.when(other)
                def _():
                    pl.semaphore_signal(barrier, inc=1, device_id=(src_row, q), device_id_type=MESH)

        @pl.when(q != col)
        def _():
            pl.semaphore_signal(barrier, inc=1, device_id=(row, q), device_id_type=MESH)

    loads = [
        pltpu.make_async_copy(linv_hbm.at[:, 0], linv, load_sem.at[0]),
        pltpu.make_async_copy(rhs_hbm.at[:, 0], rhs, load_sem.at[1]),
        pltpu.make_async_copy(pat_hbm, pat, pat_sem),
        pltpu.make_async_copy(low_hbm.at[0, 0], low.at[0], load_sem.at[2]),
        pltpu.make_async_copy(uinv_hbm.at[:, 0], uinv, load_sem.at[3]),
        pltpu.make_async_copy(low_hbm.at[1, 0], low.at[1], load_sem.at[4]),
        pltpu.make_async_copy(low_hbm.at[2, 0], low.at[2], load_sem.at[5]),
        pltpu.make_async_copy(upp_hbm.at[:, 0], upp, load_sem.at[6]),
    ]
    for copy in loads:
        copy.start()

    own_rows = pl.ds(pl.multiple_of(col * part, part), part)

    def cast_copy(rnd, step):
        source = first.at[own_rows] if rnd == 0 else slices.at[rnd]
        where = pl.ds(pl.multiple_of(place * size + col * part, part), part)
        return pltpu.make_async_remote_copy(
            src_ref=source,
            dst_ref=fetched.at[rnd, where],
            send_sem=cast_send.at[rnd],
            recv_sem=cast_recv.at[rnd],
            device_id=(target_row(step), owner_col),
            device_id_type=MESH,
        )

    def cast_local(rnd):
        source = first.at[own_rows] if rnd == 0 else slices.at[rnd]
        where = pl.ds(pl.multiple_of(place * size + col * part, part), part)
        return pltpu.make_async_copy(source, fetched.at[rnd, where], cast_recv.at[rnd])

    def cast_start(rnd):
        def one(step, unused):
            cast_copy(rnd, step).start()
            return unused

        for step in range(n_rows - 1):
            one(step, 0)

        @pl.when(jnp.logical_not(is_own))
        def _():
            cast_copy(rnd, n_rows - 1).start()

        @pl.when(is_own)
        def _():
            cast_local(rnd).start()

    def cast_wait(rnd):
        pltpu.make_async_copy(fetched.at[rnd], fetched.at[rnd], cast_recv.at[rnd]).wait()

    def cast_drain(rnd):
        def one(step, unused):
            cast_copy(rnd, step).wait_send()
            return unused

        lax.fori_loop(0, n_rows - 1, one, 0)

        @pl.when(jnp.logical_not(is_own))
        def _():
            cast_copy(rnd, n_rows - 1).wait_send()

    def peer(step):
        return lax.rem(col + step, n_cols)

    def sum_copy(rnd, step):
        q = peer(step)
        return pltpu.make_async_remote_copy(
            src_ref=prod.at[rnd, pl.ds(pl.multiple_of(q * part, part), part)],
            dst_ref=land.at[rnd, col],
            send_sem=sum_send.at[rnd],
            recv_sem=sum_recv.at[rnd],
            device_id=(row, q),
            device_id_type=MESH,
        )

    order = [4, 3, 5, 2, 6, 1, 7]

    def scatter(rnd, value):
        prod[rnd] = value.astype(BF16)
        for step in order:
            sum_copy(rnd, step).start()
        land[rnd, col] = prod[rnd, own_rows]

    def summed(rnd):
        pltpu.make_async_copy(
            land.at[rnd, pl.ds(0, n_cols - 1)], land.at[rnd, pl.ds(0, n_cols - 1)], sum_recv.at[rnd]
        ).wait()
        total = land[rnd, 0].astype(F32)
        for q in range(1, n_cols):
            total = total + land[rnd, q].astype(F32)
        return total

    def out_copy(rnd, level, step):
        return pltpu.make_async_remote_copy(
            src_ref=slices.at[rnd],
            dst_ref=out_hbm.at[level, 0, own_rows],
            send_sem=out_send.at[level],
            recv_sem=out_recv.at[level],
            device_id=(row, peer(step)),
            device_id_type=MESH,
        )

    def share(rnd, level):
        for step in order:
            out_copy(rnd, level, step).start()
        pltpu.make_async_copy(slices.at[rnd], out_hbm.at[level, 0, own_rows], out_recv.at[level]).start()

    def share_wait(rnd, level):
        pltpu.make_async_copy(out_hbm.at[level, 0], out_hbm.at[level, 0], out_recv.at[level]).wait()
        for step in order:
            out_copy(rnd, level, step).wait_send()

    def fold_lower(pair, products):
        for b in range(n_group):
            cols = slice(b * size, (b + 1) * size)
            keep = pat[pair, row, col * n_group + b].astype(F32)
            low[pair, :, cols] = (products(low[pair, :, cols]) * keep).astype(BF16)

    def fold_upper(pair, level):
        for b in range(n_group):
            cols = slice(b * size, (b + 1) * size)
            keep = pat[pair, col * n_group + b, row].astype(F32)
            upp[pair, :, cols] = (mm(uinv[level], upp[pair, :, cols]) * keep).astype(BF16)

    loads[0].wait()
    loads[1].wait()
    first[...] = mm(linv[0], rhs[0]).astype(BF16)

    pl.semaphore_wait(barrier, n_rows + n_cols - 1 - is_own.astype(jnp.int32))
    cast_start(0)

    loads[2].wait()
    loads[3].wait()
    fold_lower(0, lambda block: mm(linv[1], block))
    base1[...] = mm(linv[1], rhs[1])
    loads[4].wait()
    both = mm(uinv[2], linv[2])
    n_hi[...] = both.astype(BF16)
    n_lo[...] = (both - n_hi[...].astype(F32)).astype(BF16)

    def through(block):
        return mm(n_hi[...], block) + mm(n_lo[...], block)

    base2[...] = through(rhs[2])
    base0[...] = mm(uinv[0], first[...])
    loads[5].wait()
    fold_lower(1, through)
    loads[6].wait()
    fold_lower(2, through)

    cast_wait(0)
    scatter(0, mm(low[0], fetched[0]))
    slices[1] = (base1[own_rows] - summed(0)).astype(BF16)
    cast_start(1)
    carry[...] = mm(low[1], fetched[0])

    loads[7].wait()
    fold_upper(2, 1)
    fold_upper(1, 0)
    fold_upper(0, 0)
    padded[...] = jnp.zeros_like(padded)
    padded[own_rows] = slices[1]

    cast_wait(1)
    scatter(1, carry[...] + mm(low[2], fetched[1]))
    slices[2] = (base2[own_rows] - summed(1)).astype(BF16)
    cast_start(2)
    share(2, 2)
    carry[...] = mm(uinv[1], padded[...])

    cast_wait(2)
    scatter(2, mm(upp[2], fetched[2]) - carry[...])
    slices[3] = (-summed(2)).astype(BF16)
    cast_start(3)
    share(3, 1)
    carry[...] = mm(upp[1], fetched[2])

    cast_wait(3)
    scatter(3, carry[...] + mm(upp[0], fetched[3]))
    slices[4] = (base0[own_rows] - summed(3)).astype(BF16)
    share(4, 0)

    for rnd in range(4):
        cast_drain(rnd)
        for step in order:
            sum_copy(rnd, step).wait_send()
    share_wait(2, 2)
    share_wait(3, 1)
    share_wait(4, 0)


def solution(mesh):
    n_rows, n_cols = mesh.shape["prow"], mesh.shape["pcol"]

    def body(right_side, lower_blocks, upper_blocks, lower_inverse, upper_inverse, pattern):
        levels, _, size, width = right_side.shape
        pairs, _, _, span = lower_blocks.shape
        n_group = span // size
        part = size // n_cols
        any_spec = pl.BlockSpec(memory_space=pl.ANY)
        return pl.pallas_call(
            functools.partial(kernel, n_rows, n_cols, n_group),
            out_shape=jax.ShapeDtypeStruct((levels, 1, size, width), BF16),
            in_specs=[pl.BlockSpec(memory_space=pltpu.HBM)] * 6,
            out_specs=any_spec,
            scratch_shapes=[
                pltpu.VMEM((levels, size, width), BF16),
                pltpu.VMEM((pairs, size, span), BF16),
                pltpu.VMEM((pairs, size, span), BF16),
                pltpu.VMEM((levels, size, size), BF16),
                pltpu.VMEM((levels, size, size), BF16),
                pltpu.SMEM(pattern.shape, jnp.int32),
                pltpu.VMEM((size, width), BF16),
                pltpu.VMEM((size, width), F32),
                pltpu.VMEM((size, width), F32),
                pltpu.VMEM((size, width), F32),
                pltpu.VMEM((size, width), F32),
                pltpu.VMEM((4, size, width), BF16),
                pltpu.VMEM((4, n_cols, part, width), BF16),
                pltpu.VMEM((5, part, width), BF16),
                pltpu.VMEM((4, span, width), BF16),
                pltpu.VMEM((size, width), BF16),
                pltpu.VMEM((size, size), BF16),
                pltpu.VMEM((size, size), BF16),
                pltpu.SemaphoreType.DMA((7,)),
                pltpu.SemaphoreType.DMA(()),
                pltpu.SemaphoreType.DMA((4,)),
                pltpu.SemaphoreType.DMA((4,)),
                pltpu.SemaphoreType.DMA((4,)),
                pltpu.SemaphoreType.DMA((4,)),
                pltpu.SemaphoreType.DMA((3,)),
                pltpu.SemaphoreType.DMA((3,)),
            ],
            compiler_params=pltpu.CompilerParams(collective_id=0, has_side_effects=True, vmem_limit_bytes=24 * 1024 * 1024),
        )(*[pltpu.with_memory_space_constraint(x, pltpu.HBM) for x in (right_side, lower_blocks, upper_blocks, lower_inverse, upper_inverse, pattern)])

    placed = (
        P(None, "prow", None, None),
        P(None, "prow", None, "pcol"),
        P(None, "prow", None, "pcol"),
        P(None, "prow", None, None),
        P(None, "prow", None, None),
        P(),
    )
    return jax.shard_map(
        body, mesh=mesh, in_specs=placed, out_specs=P(None, "prow", None, None), check_vma=False
    )
```

```python
import functools

import jax
import jax.numpy as jnp
from jax import lax
from jax.experimental import pallas as pl
from jax.experimental.pallas import tpu as pltpu
from jax.sharding import PartitionSpec as P

MESH = pl.DeviceIdType.MESH
F32 = jnp.float32
BF16 = jnp.bfloat16


def mm(a, b):
    return jnp.dot(a, b, preferred_element_type=F32)


def kernel(
    n_rows, n_cols, n_group,
    rhs_hbm, low_hbm, upp_hbm, linv_hbm, uinv_hbm, pat_hbm,
    out_hbm,
    rhs, low, upp, linv, uinv, pat,
    first, base1, base2, base0, carry, prod, land, slices, fetched, padded, n_hi, n_lo,
    prod_f32, load_sem, pat_sem, cast_send, cast_recv, pass_send, pass_recv, sum_send, sum_recv, out_send, out_recv,
):
    size = rhs.shape[1]
    part = size // n_cols
    row = lax.axis_index("prow")
    col = lax.axis_index("pcol")
    owner_col = row // n_group
    place = row % n_group
    n_outer = n_rows // n_group

    barrier = pltpu.get_barrier_semaphore()

    near_order = [n_group // 2] + [d for d in range(1, n_group) if d != n_group // 2]
    outer_order = [4, 3, 5, 2, 6, 1, 7]

    def beside(step):
        return owner_col * n_group + (place + step) % n_group

    def across(step):
        return (owner_col + step) % n_outer * n_group + place

    is_own = owner_col == col

    for q in range(n_cols):
        src_row = col * n_group + place

        @pl.when(jnp.logical_or(src_row != row, q != col))
        def _():
            pl.semaphore_signal(barrier, inc=1, device_id=(src_row, q), device_id_type=MESH)

        @pl.when(q != col)
        def _():
            pl.semaphore_signal(barrier, inc=1, device_id=(row, q), device_id_type=MESH)

    for step in near_order:
        pl.semaphore_signal(barrier, inc=1, device_id=(beside(step), col), device_id_type=MESH)

    loads = [
        pltpu.make_async_copy(linv_hbm.at[:, 0], linv, load_sem.at[0]),
        pltpu.make_async_copy(rhs_hbm.at[:, 0], rhs, load_sem.at[1]),
        pltpu.make_async_copy(pat_hbm, pat, pat_sem),
        pltpu.make_async_copy(low_hbm.at[0, 0], low.at[0], load_sem.at[2]),
        pltpu.make_async_copy(uinv_hbm.at[:, 0], uinv, load_sem.at[3]),
        pltpu.make_async_copy(low_hbm.at[1, 0], low.at[1], load_sem.at[4]),
        pltpu.make_async_copy(low_hbm.at[2, 0], low.at[2], load_sem.at[5]),
        pltpu.make_async_copy(upp_hbm.at[:, 0], upp, load_sem.at[6]),
    ]
    for copy in loads:
        copy.start()

    own_rows = pl.ds(pl.multiple_of(col * part, part), part)

    block_rows = pl.ds(pl.multiple_of(place * size, size), size)

    def cast_ends(rnd):
        source = first.at[own_rows] if rnd == 0 else slices.at[rnd]
        return source, fetched.at[rnd, pl.ds(pl.multiple_of(place * size + col * part, part), part)]

    def cast_copy(rnd, step):
        source, target = cast_ends(rnd)
        return pltpu.make_async_remote_copy(
            src_ref=source,
            dst_ref=target,
            send_sem=cast_send.at[rnd],
            recv_sem=cast_recv.at[rnd, col],
            device_id=(across(step), owner_col),
            device_id_type=MESH,
        )

    def cast_start(rnd):
        for step in outer_order:
            cast_copy(rnd, step).start()

        @pl.when(jnp.logical_not(is_own))
        def _():
            cast_copy(rnd, 0).start()

        @pl.when(is_own)
        def _():
            source, target = cast_ends(rnd)
            pltpu.make_async_copy(source, target, cast_recv.at[rnd, col]).start()

    def pass_copy(rnd, chip, step):
        rows = fetched.at[rnd, pl.ds(pl.multiple_of(place * size + chip * 2 * part, part), 2 * part)]
        return pltpu.make_async_remote_copy(
            src_ref=rows,
            dst_ref=rows,
            send_sem=pass_send.at[rnd],
            recv_sem=pass_recv.at[rnd, step],
            device_id=(beside(step), col),
            device_id_type=MESH,
        )

    def chip_at(d):
        return (col // 2 + d) % (n_cols // 2)

    def relay(rnd):
        for d in (0, 1, 3, 2):
            chip = chip_at(d)
            for k in range(2):
                q = chip * 2 + k
                rows = fetched.at[rnd, pl.ds(pl.multiple_of(place * size + q * part, part), part)]
                pltpu.make_async_copy(rows, rows, cast_recv.at[rnd, q]).wait()
            for step in near_order:
                pass_copy(rnd, chip, step).start()

    def product(rnd, matrix):
        def piece(offset):
            where = pl.ds(pl.multiple_of((place + offset) % n_group * size, size), size)
            return mm(matrix[:, where], fetched[rnd, where])

        prod_f32[...] = piece(0)
        for step in (1, 3, 2):
            where = pl.ds(pl.multiple_of((place + n_group - step) % n_group * size, size), size)
            pltpu.make_async_copy(fetched.at[rnd, where], fetched.at[rnd, where], pass_recv.at[rnd, step]).wait()
            prod_f32[...] += piece(n_group - step)
        return prod_f32[...]

    def cast_drain(rnd):
        for step in outer_order:
            cast_copy(rnd, step).wait_send()

        @pl.when(jnp.logical_not(is_own))
        def _():
            cast_copy(rnd, 0).wait_send()

        for d in range(n_cols // 2):
            for step in near_order:
                pass_copy(rnd, d, step).wait_send()

    def peer(step):
        return lax.rem(col + step, n_cols)

    def sum_copy(rnd, step):
        q = peer(step)
        return pltpu.make_async_remote_copy(
            src_ref=prod.at[rnd, pl.ds(pl.multiple_of(q * part, part), part)],
            dst_ref=land.at[rnd, col],
            send_sem=sum_send.at[rnd],
            recv_sem=sum_recv.at[rnd],
            device_id=(row, q),
            device_id_type=MESH,
        )

    order = [4, 3, 5, 2, 6, 1, 7]

    def scatter(rnd, value):
        prod[rnd] = value.astype(BF16)
        for step in order:
            sum_copy(rnd, step).start()
        land[rnd, col] = prod[rnd, own_rows]

    def summed(rnd):
        pltpu.make_async_copy(
            land.at[rnd, pl.ds(0, n_cols - 1)], land.at[rnd, pl.ds(0, n_cols - 1)], sum_recv.at[rnd]
        ).wait()
        total = land[rnd, 0].astype(F32)
        for q in range(1, n_cols):
            total = total + land[rnd, q].astype(F32)
        return total

    def out_copy(rnd, level, step):
        return pltpu.make_async_remote_copy(
            src_ref=slices.at[rnd],
            dst_ref=out_hbm.at[level, 0, own_rows],
            send_sem=out_send.at[level],
            recv_sem=out_recv.at[level],
            device_id=(row, peer(step)),
            device_id_type=MESH,
        )

    def share(rnd, level):
        for step in order:
            out_copy(rnd, level, step).start()
        pltpu.make_async_copy(slices.at[rnd], out_hbm.at[level, 0, own_rows], out_recv.at[level]).start()

    def share_wait(rnd, level):
        pltpu.make_async_copy(out_hbm.at[level, 0], out_hbm.at[level, 0], out_recv.at[level]).wait()
        for step in order:
            out_copy(rnd, level, step).wait_send()

    def fold_lower(pair, products):
        for b in range(n_group):
            cols = slice(b * size, (b + 1) * size)
            keep = pat[pair, row, col * n_group + b].astype(F32)
            low[pair, :, cols] = (products(low[pair, :, cols]) * keep).astype(BF16)

    def fold_upper(pair, level):
        for b in range(n_group):
            cols = slice(b * size, (b + 1) * size)
            keep = pat[pair, col * n_group + b, row].astype(F32)
            upp[pair, :, cols] = (mm(uinv[level], upp[pair, :, cols]) * keep).astype(BF16)

    loads[0].wait()
    loads[1].wait()
    first[...] = mm(linv[0], rhs[0]).astype(BF16)

    pl.semaphore_wait(barrier, n_outer + n_group - 1 + n_cols - 1 - is_own.astype(jnp.int32))
    cast_start(0)

    loads[2].wait()
    loads[3].wait()
    fold_lower(0, lambda block: mm(linv[1], block))
    base1[...] = mm(linv[1], rhs[1])
    loads[4].wait()
    both = mm(uinv[2], linv[2])
    n_hi[...] = both.astype(BF16)
    n_lo[...] = (both - n_hi[...].astype(F32)).astype(BF16)

    def through(block):
        return mm(n_hi[...], block) + mm(n_lo[...], block)

    base2[...] = through(rhs[2])
    base0[...] = mm(uinv[0], first[...])
    loads[5].wait()
    fold_lower(1, through)
    loads[6].wait()
    fold_lower(2, through)

    relay(0)
    scatter(0, product(0, low.at[0]))
    slices[1] = (base1[own_rows] - summed(0)).astype(BF16)
    cast_start(1)
    carry[...] = mm(low[1], fetched[0])

    loads[7].wait()
    fold_upper(2, 1)
    fold_upper(1, 0)
    fold_upper(0, 0)
    padded[...] = jnp.zeros_like(padded)
    padded[own_rows] = slices[1]

    relay(1)
    scatter(1, carry[...] + product(1, low.at[2]))
    slices[2] = (base2[own_rows] - summed(1)).astype(BF16)
    cast_start(2)
    share(2, 2)
    carry[...] = mm(uinv[1], padded[...])

    relay(2)
    scatter(2, product(2, upp.at[2]) - carry[...])
    slices[3] = (-summed(2)).astype(BF16)
    cast_start(3)
    share(3, 1)
    carry[...] = mm(upp[1], fetched[2])

    relay(3)
    scatter(3, carry[...] + product(3, upp.at[0]))
    slices[4] = (base0[own_rows] - summed(3)).astype(BF16)
    share(4, 0)

    for rnd in range(4):
        cast_drain(rnd)
        for step in order:
            sum_copy(rnd, step).wait_send()
    share_wait(2, 2)
    share_wait(3, 1)
    share_wait(4, 0)


def solution(mesh):
    n_rows, n_cols = mesh.shape["prow"], mesh.shape["pcol"]

    def body(right_side, lower_blocks, upper_blocks, lower_inverse, upper_inverse, pattern):
        levels, _, size, width = right_side.shape
        pairs, _, _, span = lower_blocks.shape
        n_group = span // size
        part = size // n_cols
        any_spec = pl.BlockSpec(memory_space=pl.ANY)
        return pl.pallas_call(
            functools.partial(kernel, n_rows, n_cols, n_group),
            out_shape=jax.ShapeDtypeStruct((levels, 1, size, width), BF16),
            in_specs=[pl.BlockSpec(memory_space=pltpu.HBM)] * 6,
            out_specs=any_spec,
            scratch_shapes=[
                pltpu.VMEM((levels, size, width), BF16),
                pltpu.VMEM((pairs, size, span), BF16),
                pltpu.VMEM((pairs, size, span), BF16),
                pltpu.VMEM((levels, size, size), BF16),
                pltpu.VMEM((levels, size, size), BF16),
                pltpu.SMEM(pattern.shape, jnp.int32),
                pltpu.VMEM((size, width), BF16),
                pltpu.VMEM((size, width), F32),
                pltpu.VMEM((size, width), F32),
                pltpu.VMEM((size, width), F32),
                pltpu.VMEM((size, width), F32),
                pltpu.VMEM((4, size, width), BF16),
                pltpu.VMEM((4, n_cols, part, width), BF16),
                pltpu.VMEM((5, part, width), BF16),
                pltpu.VMEM((4, span, width), BF16),
                pltpu.VMEM((size, width), BF16),
                pltpu.VMEM((size, size), BF16),
                pltpu.VMEM((size, size), BF16),
                pltpu.VMEM((size, width), F32),
                pltpu.SemaphoreType.DMA((7,)),
                pltpu.SemaphoreType.DMA(()),
                pltpu.SemaphoreType.DMA((4,)),
                pltpu.SemaphoreType.DMA((4, n_cols)),
                pltpu.SemaphoreType.DMA((4,)),
                pltpu.SemaphoreType.DMA((4, n_group)),
                pltpu.SemaphoreType.DMA((4,)),
                pltpu.SemaphoreType.DMA((4,)),
                pltpu.SemaphoreType.DMA((3,)),
                pltpu.SemaphoreType.DMA((3,)),
            ],
            compiler_params=pltpu.CompilerParams(collective_id=0, has_side_effects=True, vmem_limit_bytes=24 * 1024 * 1024),
        )(*[pltpu.with_memory_space_constraint(x, pltpu.HBM) for x in (right_side, lower_blocks, upper_blocks, lower_inverse, upper_inverse, pattern)])

    placed = (
        P(None, "prow", None, None),
        P(None, "prow", None, "pcol"),
        P(None, "prow", None, "pcol"),
        P(None, "prow", None, None),
        P(None, "prow", None, None),
        P(),
    )
    return jax.shard_map(
        body, mesh=mesh, in_specs=placed, out_specs=P(None, "prow", None, None), check_vma=False
    )
```

```python
import functools

import jax
import jax.numpy as jnp
from jax import lax
from jax.experimental import pallas as pl
from jax.experimental.pallas import tpu as pltpu
from jax.sharding import PartitionSpec as P

MESH = pl.DeviceIdType.MESH
F32 = jnp.float32
BF16 = jnp.bfloat16


def mm(a, b):
    return jnp.dot(a, b, preferred_element_type=F32)


def kernel(
    n_rows, n_cols, n_group,
    rhs_hbm, low_hbm, upp_hbm, linv_hbm, uinv_hbm, pat_hbm,
    out_hbm,
    rhs, low, upp, linv, uinv, pat,
    first, base1, base2, base0, carry, prod, land, slices, fetched, passing, padded, n_hi, n_lo,
    prod_f32, load_sem, pat_sem, cast_send, cast_recv, pass_send, pass_recv, sum_send, sum_recv, out_send, out_recv,
):
    size = rhs.shape[1]
    part = size // n_cols
    row = lax.axis_index("prow")
    col = lax.axis_index("pcol")
    owner_col = row // n_group
    place = row % n_group
    n_outer = n_rows // n_group

    barrier = pltpu.get_barrier_semaphore()

    near_order = [n_group // 2] + [d for d in range(1, n_group) if d != n_group // 2]
    outer_order = [4, 3, 5, 2, 6, 1, 7]

    def beside(step):
        return owner_col * n_group + (place + step) % n_group

    def across(step):
        return (owner_col + step) % n_outer * n_group + place


    for step in outer_order:
        pl.semaphore_signal(barrier, inc=1, device_id=(across(step), col), device_id_type=MESH)
    for step in near_order + [0]:
        for turn in range(n_cols):
            if step or turn:
                other = (beside(step), (col + turn) % n_cols)
                pl.semaphore_signal(barrier, inc=1, device_id=other, device_id_type=MESH)

    loads = [
        pltpu.make_async_copy(linv_hbm.at[:, 0], linv, load_sem.at[0]),
        pltpu.make_async_copy(rhs_hbm.at[:, 0], rhs, load_sem.at[1]),
        pltpu.make_async_copy(pat_hbm, pat, pat_sem),
        pltpu.make_async_copy(low_hbm.at[0, 0], low.at[0], load_sem.at[2]),
        pltpu.make_async_copy(uinv_hbm.at[:, 0], uinv, load_sem.at[3]),
        pltpu.make_async_copy(low_hbm.at[1, 0], low.at[1], load_sem.at[4]),
        pltpu.make_async_copy(low_hbm.at[2, 0], low.at[2], load_sem.at[5]),
        pltpu.make_async_copy(upp_hbm.at[:, 0], upp, load_sem.at[6]),
    ]
    for copy in loads:
        copy.start()

    own_rows = pl.ds(pl.multiple_of(col * part, part), part)

    def cast_source(rnd):
        return first.at[own_rows] if rnd == 0 else slices.at[rnd]

    def cast_copy(rnd, step):
        return pltpu.make_async_remote_copy(
            src_ref=cast_source(rnd),
            dst_ref=passing.at[rnd, owner_col],
            send_sem=cast_send.at[rnd],
            recv_sem=cast_recv.at[rnd, owner_col],
            device_id=(across(step), col),
            device_id_type=MESH,
        )

    def pass_ends(rnd, d):
        plane = (owner_col + d) % n_outer
        source = cast_source(rnd) if d == 0 else passing.at[rnd, plane]
        target = fetched.at[rnd, pl.ds(pl.multiple_of(place * size + col * part, part), part)]
        return plane, source, target

    def pass_copy(rnd, d, step):
        plane, source, target = pass_ends(rnd, d)
        return pltpu.make_async_remote_copy(
            src_ref=source,
            dst_ref=target,
            send_sem=pass_send.at[rnd],
            recv_sem=pass_recv.at[rnd, step],
            device_id=(beside(step), plane),
            device_id_type=MESH,
        )

    def pass_on(rnd, d):
        plane, source, target = pass_ends(rnd, d)
        for step in near_order:
            pass_copy(rnd, d, step).start()

        @pl.when(plane != col)
        def _():
            pass_copy(rnd, d, 0).start()

        @pl.when(plane == col)
        def _():
            pltpu.make_async_copy(source, target, pass_recv.at[rnd, 0]).start()

    def cast_start(rnd):
        for step in outer_order:
            cast_copy(rnd, step).start()
        pass_on(rnd, 0)

    def relay(rnd):
        for d in (1, 7, 2, 6, 3, 5, 4):
            plane, source, target = pass_ends(rnd, d)
            pltpu.make_async_copy(source, source, cast_recv.at[rnd, plane]).wait()
            pass_on(rnd, d)

    def product(rnd, matrix):
        def piece(offset):
            where = pl.ds(pl.multiple_of((place + offset) % n_group * size, size), size)
            return mm(matrix[:, where], fetched[rnd, where])

        for step in (0, 1, 3, 2):
            where = pl.ds(pl.multiple_of((place + n_group - step) % n_group * size, size), size)
            pltpu.make_async_copy(fetched.at[rnd, where], fetched.at[rnd, where], pass_recv.at[rnd, step]).wait()
            if step:
                prod_f32[...] += piece(n_group - step)
            else:
                prod_f32[...] = piece(0)
        return prod_f32[...]

    def cast_drain(rnd):
        for step in outer_order:
            cast_copy(rnd, step).wait_send()
        for d in range(n_outer):
            plane, source, target = pass_ends(rnd, d)
            for step in near_order:
                pass_copy(rnd, d, step).wait_send()

            @pl.when(plane != col)
            def _():
                pass_copy(rnd, d, 0).wait_send()

    def peer(step):
        return lax.rem(col + step, n_cols)

    def sum_copy(rnd, step):
        q = peer(step)
        return pltpu.make_async_remote_copy(
            src_ref=prod.at[rnd, pl.ds(pl.multiple_of(q * part, part), part)],
            dst_ref=land.at[rnd, col],
            send_sem=sum_send.at[rnd],
            recv_sem=sum_recv.at[rnd],
            device_id=(row, q),
            device_id_type=MESH,
        )

    order = [4, 3, 5, 2, 6, 1, 7]

    def scatter(rnd, value):
        prod[rnd] = value.astype(BF16)
        for step in order:
            sum_copy(rnd, step).start()
        land[rnd, col] = prod[rnd, own_rows]

    def summed(rnd):
        pltpu.make_async_copy(
            land.at[rnd, pl.ds(0, n_cols - 1)], land.at[rnd, pl.ds(0, n_cols - 1)], sum_recv.at[rnd]
        ).wait()
        total = land[rnd, 0].astype(F32)
        for q in range(1, n_cols):
            total = total + land[rnd, q].astype(F32)
        return total

    def out_copy(rnd, level, step):
        return pltpu.make_async_remote_copy(
            src_ref=slices.at[rnd],
            dst_ref=out_hbm.at[level, 0, own_rows],
            send_sem=out_send.at[level],
            recv_sem=out_recv.at[level],
            device_id=(row, peer(step)),
            device_id_type=MESH,
        )

    def share(rnd, level):
        for step in order:
            out_copy(rnd, level, step).start()
        pltpu.make_async_copy(slices.at[rnd], out_hbm.at[level, 0, own_rows], out_recv.at[level]).start()

    def share_wait(rnd, level):
        pltpu.make_async_copy(out_hbm.at[level, 0], out_hbm.at[level, 0], out_recv.at[level]).wait()
        for step in order:
            out_copy(rnd, level, step).wait_send()

    def fold_lower(pair, products):
        for b in range(n_group):
            cols = slice(b * size, (b + 1) * size)
            keep = pat[pair, row, col * n_group + b].astype(F32)
            low[pair, :, cols] = (products(low[pair, :, cols]) * keep).astype(BF16)

    def fold_upper(pair, level):
        for b in range(n_group):
            cols = slice(b * size, (b + 1) * size)
            keep = pat[pair, col * n_group + b, row].astype(F32)
            upp[pair, :, cols] = (mm(uinv[level], upp[pair, :, cols]) * keep).astype(BF16)

    loads[0].wait()
    loads[1].wait()
    first[...] = mm(linv[0], rhs[0]).astype(BF16)

    pl.semaphore_wait(barrier, n_outer - 1 + n_group * n_cols - 1)
    cast_start(0)

    loads[2].wait()
    loads[3].wait()
    fold_lower(0, lambda block: mm(linv[1], block))
    base1[...] = mm(linv[1], rhs[1])
    loads[4].wait()
    both = mm(uinv[2], linv[2])
    n_hi[...] = both.astype(BF16)
    n_lo[...] = (both - n_hi[...].astype(F32)).astype(BF16)

    def through(block):
        return mm(n_hi[...], block) + mm(n_lo[...], block)

    base2[...] = through(rhs[2])
    base0[...] = mm(uinv[0], first[...])
    loads[5].wait()
    fold_lower(1, through)
    loads[6].wait()
    fold_lower(2, through)

    relay(0)
    scatter(0, product(0, low.at[0]))
    slices[1] = (base1[own_rows] - summed(0)).astype(BF16)
    cast_start(1)
    carry[...] = mm(low[1], fetched[0])

    loads[7].wait()
    fold_upper(2, 1)
    fold_upper(1, 0)
    fold_upper(0, 0)
    padded[...] = jnp.zeros_like(padded)
    padded[own_rows] = slices[1]

    relay(1)
    scatter(1, carry[...] + product(1, low.at[2]))
    slices[2] = (base2[own_rows] - summed(1)).astype(BF16)
    cast_start(2)
    share(2, 2)
    carry[...] = mm(uinv[1], padded[...])

    relay(2)
    scatter(2, product(2, upp.at[2]) - carry[...])
    slices[3] = (-summed(2)).astype(BF16)
    cast_start(3)
    share(3, 1)
    carry[...] = mm(upp[1], fetched[2])

    relay(3)
    scatter(3, carry[...] + product(3, upp.at[0]))
    slices[4] = (base0[own_rows] - summed(3)).astype(BF16)
    share(4, 0)

    for rnd in range(4):
        cast_drain(rnd)
        for step in order:
            sum_copy(rnd, step).wait_send()
    share_wait(2, 2)
    share_wait(3, 1)
    share_wait(4, 0)


def solution(mesh):
    n_rows, n_cols = mesh.shape["prow"], mesh.shape["pcol"]

    def body(right_side, lower_blocks, upper_blocks, lower_inverse, upper_inverse, pattern):
        levels, _, size, width = right_side.shape
        pairs, _, _, span = lower_blocks.shape
        n_group = span // size
        part = size // n_cols
        any_spec = pl.BlockSpec(memory_space=pl.ANY)
        return pl.pallas_call(
            functools.partial(kernel, n_rows, n_cols, n_group),
            out_shape=jax.ShapeDtypeStruct((levels, 1, size, width), BF16),
            in_specs=[pl.BlockSpec(memory_space=pltpu.HBM)] * 6,
            out_specs=any_spec,
            scratch_shapes=[
                pltpu.VMEM((levels, size, width), BF16),
                pltpu.VMEM((pairs, size, span), BF16),
                pltpu.VMEM((pairs, size, span), BF16),
                pltpu.VMEM((levels, size, size), BF16),
                pltpu.VMEM((levels, size, size), BF16),
                pltpu.SMEM(pattern.shape, jnp.int32),
                pltpu.VMEM((size, width), BF16),
                pltpu.VMEM((size, width), F32),
                pltpu.VMEM((size, width), F32),
                pltpu.VMEM((size, width), F32),
                pltpu.VMEM((size, width), F32),
                pltpu.VMEM((4, size, width), BF16),
                pltpu.VMEM((4, n_cols, part, width), BF16),
                pltpu.VMEM((5, part, width), BF16),
                pltpu.VMEM((4, span, width), BF16),
                pltpu.VMEM((4, n_rows // n_group, part, width), BF16),
                pltpu.VMEM((size, width), BF16),
                pltpu.VMEM((size, size), BF16),
                pltpu.VMEM((size, size), BF16),
                pltpu.VMEM((size, width), F32),
                pltpu.SemaphoreType.DMA((7,)),
                pltpu.SemaphoreType.DMA(()),
                pltpu.SemaphoreType.DMA((4,)),
                pltpu.SemaphoreType.DMA((4, n_rows // n_group)),
                pltpu.SemaphoreType.DMA((4,)),
                pltpu.SemaphoreType.DMA((4, n_group)),
                pltpu.SemaphoreType.DMA((4,)),
                pltpu.SemaphoreType.DMA((4,)),
                pltpu.SemaphoreType.DMA((3,)),
                pltpu.SemaphoreType.DMA((3,)),
            ],
            compiler_params=pltpu.CompilerParams(collective_id=0, has_side_effects=True, vmem_limit_bytes=24 * 1024 * 1024),
        )(*[pltpu.with_memory_space_constraint(x, pltpu.HBM) for x in (right_side, lower_blocks, upper_blocks, lower_inverse, upper_inverse, pattern)])

    placed = (
        P(None, "prow", None, None),
        P(None, "prow", None, "pcol"),
        P(None, "prow", None, "pcol"),
        P(None, "prow", None, None),
        P(None, "prow", None, None),
        P(),
    )
    return jax.shard_map(
        body, mesh=mesh, in_specs=placed, out_specs=P(None, "prow", None, None), check_vma=False
    )
```

```python
import functools

import jax
import jax.numpy as jnp
from jax import lax
from jax.experimental import pallas as pl
from jax.experimental.pallas import tpu as pltpu
from jax.sharding import PartitionSpec as P

MESH = pl.DeviceIdType.MESH
F32 = jnp.float32
BF16 = jnp.bfloat16
HALVES = 2
SUM_TYPE = BF16


def mm(a, b):
    return jnp.dot(a, b, preferred_element_type=F32)


def mm_t(a, b):
    return lax.dot_general(a, b, (((1,), (1,)), ((), ())), preferred_element_type=F32)


def kernel(
    n_rows, n_cols, n_group,
    rhs_hbm, low_hbm, upp_hbm, linv_hbm, uinv_hbm, pat_hbm,
    out_hbm,
    rhs, low, upp, linv, uinv, pat, low_t, upp_t,
    first, base1, base2, base0, base3, carry, prod, land, slices, fetched, n_hi, n_lo,
    load_sem, pat_sem, cast_send, cast_recv, sum_send, sum_recv, out_send, out_recv,
):
    size = rhs.shape[1]
    width = rhs.shape[2]
    part = width // n_cols
    n_chips = n_cols // HALVES
    half_rows = width // HALVES
    row = lax.axis_index("prow")
    col = lax.axis_index("pcol")
    core = lax.rem(col, HALVES)
    chip = col // HALVES
    owner_col = row // n_group
    place = row % n_group
    n_outer = n_rows // n_group
    is_own = owner_col == col

    barrier = pltpu.get_barrier_semaphore()
    for q in range(n_cols):
        for b in range(n_group):
            src_row = col * n_group + b

            @pl.when(jnp.logical_or(src_row != row, q != col))
            def _():
                pl.semaphore_signal(barrier, inc=1, device_id=(src_row, q), device_id_type=MESH)

        @pl.when(q != col)
        def _():
            pl.semaphore_signal(barrier, inc=1, device_id=(row, q), device_id_type=MESH)

    loads = [
        pltpu.make_async_copy(linv_hbm.at[:, 0], linv, load_sem.at[0]),
        pltpu.make_async_copy(rhs_hbm.at[:, 0], rhs, load_sem.at[1]),
        pltpu.make_async_copy(pat_hbm, pat, pat_sem),
        pltpu.make_async_copy(low_hbm.at[0, 0], low.at[0], load_sem.at[2]),
        pltpu.make_async_copy(uinv_hbm.at[:, 0], uinv, load_sem.at[3]),
        pltpu.make_async_copy(low_hbm.at[1, 0], low.at[1], load_sem.at[4]),
        pltpu.make_async_copy(low_hbm.at[2, 0], low.at[2], load_sem.at[5]),
        pltpu.make_async_copy(upp_hbm.at[:, 0], upp, load_sem.at[6]),
    ]
    for copy in loads:
        copy.start()

    own = pl.ds(pl.multiple_of(core * half_rows + chip * part, part), part)
    in_half = pl.ds(pl.multiple_of(chip * part, part), part)
    in_span = pl.ds(pl.multiple_of(place * size, size), size)

    def target_row(step):
        i, j = step // n_group, step % n_group
        d_outer = n_outer // 2 + ((i + 1) // 2) * (1 - 2 * (i % 2))
        d_inner = n_group // 2 + ((j + 1) // 2) * (1 - 2 * (j % 2))
        outer = (row // n_group + d_outer) % n_outer
        inner = (row % n_group + d_inner) % n_group
        return outer * n_group + inner

    def cast_ends(rnd):
        source = first.at[own] if rnd == 0 else slices.at[rnd]
        return source, fetched.at[rnd, core, in_half, in_span]

    def cast_copy(rnd, step):
        source, target = cast_ends(rnd)
        return pltpu.make_async_remote_copy(
            src_ref=source,
            dst_ref=target,
            send_sem=cast_send.at[rnd],
            recv_sem=cast_recv.at[rnd, core],
            device_id=(target_row(step), owner_col),
            device_id_type=MESH,
        )

    def cast_start(rnd):
        def one(step, unused):
            cast_copy(rnd, step).start()
            return unused

        lax.fori_loop(0, n_rows - 1, one, 0)

        @pl.when(jnp.logical_not(is_own))
        def _():
            cast_copy(rnd, n_rows - 1).start()

        @pl.when(is_own)
        def _():
            source, target = cast_ends(rnd)
            pltpu.make_async_copy(source, target, cast_recv.at[rnd, core]).start()

    def cast_wait(rnd, half):
        whole = fetched.at[rnd, half]
        pltpu.make_async_copy(whole, whole, cast_recv.at[rnd, half]).wait()

    def cast_drain(rnd):
        def one(step, unused):
            cast_copy(rnd, step).wait_send()
            return unused

        lax.fori_loop(0, n_rows - 1, one, 0)

        @pl.when(jnp.logical_not(is_own))
        def _():
            cast_copy(rnd, n_rows - 1).wait_send()

    def sum_copy(rnd, half, other):
        return pltpu.make_async_remote_copy(
            src_ref=prod.at[rnd, half, pl.ds(pl.multiple_of(other * part, part), part)],
            dst_ref=land.at[rnd, col],
            send_sem=sum_send.at[rnd, half],
            recv_sem=sum_recv.at[rnd],
            device_id=(row, other * HALVES + half),
            device_id_type=MESH,
        )

    chip_order = [n_chips // 2] + [d for d in range(1, n_chips) if d != n_chips // 2]

    def scatter(rnd, half, value):
        prod[rnd, half] = value.astype(prod.dtype)
        for step in chip_order:
            sum_copy(rnd, half, lax.rem(chip + step, n_chips)).start()

        @pl.when(core != half)
        def _():
            sum_copy(rnd, half, chip).start()

    def scatter_drain(rnd, half):
        for step in chip_order:
            sum_copy(rnd, half, lax.rem(chip + step, n_chips)).wait_send()

        @pl.when(core != half)
        def _():
            sum_copy(rnd, half, chip).wait_send()

    def summed(rnd, half):
        land[rnd, col] = prod[rnd, half, in_half]
        most = land.at[rnd, pl.ds(0, n_cols - 1)]
        pltpu.make_async_copy(most, most, sum_recv.at[rnd]).wait()
        total = land[rnd, 0].astype(F32)
        for q in range(1, n_cols):
            total = total + land[rnd, q].astype(F32)
        return total

    def out_copy(rnd, level, step):
        return pltpu.make_async_remote_copy(
            src_ref=slices.at[rnd],
            dst_ref=out_hbm.at[level, own],
            send_sem=out_send.at[level],
            recv_sem=out_recv.at[level],
            device_id=(row, lax.rem(col + step, n_cols)),
            device_id_type=MESH,
        )

    peer_order = [4, 3, 5, 2, 6, 1, 7]

    def share(rnd, level):
        for step in peer_order:
            out_copy(rnd, level, step).start()
        pltpu.make_async_copy(slices.at[rnd], out_hbm.at[level, own], out_recv.at[level]).start()

    def share_wait(rnd, level):
        whole = out_hbm.at[level]
        pltpu.make_async_copy(whole, whole, out_recv.at[level]).wait()
        for step in peer_order:
            out_copy(rnd, level, step).wait_send()

    def fold_lower(pair, products):
        for b in range(n_group):
            cols = slice(b * size, (b + 1) * size)
            keep = pat[pair, row, col * n_group + b].astype(F32)
            low_t[pair, cols] = (products(low[pair, :, cols]) * keep).T.astype(BF16)

    def fold_upper(pair, level):
        for b in range(n_group):
            cols = slice(b * size, (b + 1) * size)
            keep = pat[pair, col * n_group + b, row].astype(F32)
            upp_t[pair, cols] = (mm(uinv[level], upp[pair, :, cols]) * keep).T.astype(BF16)

    loads[0].wait()
    loads[1].wait()
    first[...] = mm(linv[0], rhs[0]).T.astype(BF16)

    pl.semaphore_wait(barrier, n_rows + n_cols - 1 - is_own.astype(jnp.int32))

    @pl.when(core == 0)
    def _():
        cast_start(0)

    loads[2].wait()
    loads[3].wait()
    fold_lower(0, lambda block: mm(linv[1], block))
    base1[...] = mm(linv[1], rhs[1]).T
    loads[4].wait()
    both = mm(uinv[2], linv[2])
    n_hi[...] = both.astype(BF16)
    n_lo[...] = (both - n_hi[...].astype(F32)).astype(BF16)

    def through(block):
        return mm(n_hi[...], block) + mm(n_lo[...], block)

    base2[...] = through(rhs[2]).T
    base0[...] = mm_t(first[...], uinv[0])

    loads[5].wait()
    fold_lower(1, through)
    loads[6].wait()
    fold_lower(2, through)
    loads[7].wait()
    fold_upper(2, 1)
    fold_upper(1, 0)
    fold_upper(0, 0)

    @pl.when(core == 1)
    def _():
        cast_start(0)

    for rnd in range(4):
        for half in range(HALVES):
            cast_wait(rnd, half)
            got = fetched[rnd, half]
            if rnd == 0:
                value = mm(got, low_t[0])
            elif rnd == 1:
                value = mm(got, low_t[2]) + carry[half]
            elif rnd == 2:
                value = mm(got, upp_t[2])
            else:
                value = mm(got, upp_t[0]) + carry[half]
            scatter(rnd, half, value)
            if rnd == 0:
                carry[half] = mm(got, low_t[1])
            if rnd == 2:
                carry[half] = mm(got, upp_t[1])

            @pl.when(core == half)
            def _():
                base = (lambda: base1[own], lambda: base2[own], lambda: base3[...], lambda: base0[own])[rnd]()
                slices[rnd + 1] = (base - summed(rnd, half)).astype(BF16)
                if rnd < 3:
                    cast_start(rnd + 1)
                if rnd == 0:
                    base3[...] = mm_t(slices[1], uinv[1])
                else:
                    share(rnd + 1, 3 - rnd)

    for rnd in range(4):
        cast_drain(rnd)
        for half in range(HALVES):
            scatter_drain(rnd, half)
    for rnd in range(1, 4):
        share_wait(rnd + 1, 3 - rnd)


def solution(mesh):
    n_rows, n_cols = mesh.shape["prow"], mesh.shape["pcol"]

    def body(right_side, lower_blocks, upper_blocks, lower_inverse, upper_inverse, pattern):
        levels, _, size, width = right_side.shape
        pairs, _, _, span = lower_blocks.shape
        n_group = span // size
        part = width // n_cols
        half_rows = width // HALVES
        any_spec = pl.BlockSpec(memory_space=pl.ANY)
        turned = pl.pallas_call(
            functools.partial(kernel, n_rows, n_cols, n_group),
            out_shape=jax.ShapeDtypeStruct((levels, width, size), BF16),
            in_specs=[any_spec] * 6,
            out_specs=any_spec,
            scratch_shapes=[
                pltpu.VMEM((levels, size, width), BF16),
                pltpu.VMEM((pairs, size, span), BF16),
                pltpu.VMEM((pairs, size, span), BF16),
                pltpu.VMEM((levels, size, size), BF16),
                pltpu.VMEM((levels, size, size), BF16),
                pltpu.SMEM(pattern.shape, jnp.int32),
                pltpu.VMEM((pairs, span, size), BF16),
                pltpu.VMEM((pairs, span, size), BF16),
                pltpu.VMEM((width, size), BF16),
                pltpu.VMEM((width, size), F32),
                pltpu.VMEM((width, size), F32),
                pltpu.VMEM((width, size), F32),
                pltpu.VMEM((part, size), F32),
                pltpu.VMEM((HALVES, half_rows, size), F32),
                pltpu.VMEM((4, HALVES, half_rows, size), SUM_TYPE),
                pltpu.VMEM((4, n_cols, part, size), SUM_TYPE),
                pltpu.VMEM((5, part, size), BF16),
                pltpu.VMEM((4, HALVES, half_rows, span), BF16),
                pltpu.VMEM((size, size), BF16),
                pltpu.VMEM((size, size), BF16),
                pltpu.SemaphoreType.DMA((7,)),
                pltpu.SemaphoreType.DMA(()),
                pltpu.SemaphoreType.DMA((4,)),
                pltpu.SemaphoreType.DMA((4, HALVES)),
                pltpu.SemaphoreType.DMA((4, HALVES)),
                pltpu.SemaphoreType.DMA((4,)),
                pltpu.SemaphoreType.DMA((3,)),
                pltpu.SemaphoreType.DMA((3,)),
            ],
            compiler_params=pltpu.CompilerParams(collective_id=0, has_side_effects=True, vmem_limit_bytes=24 * 1024 * 1024),
        )(*[pltpu.with_memory_space_constraint(x, pltpu.HBM) for x in (right_side, lower_blocks, upper_blocks, lower_inverse, upper_inverse, pattern)])
        return jnp.swapaxes(turned, 1, 2)[:, None]

    placed = (
        P(None, "prow", None, None),
        P(None, "prow", None, "pcol"),
        P(None, "prow", None, "pcol"),
        P(None, "prow", None, None),
        P(None, "prow", None, None),
        P(),
    )
    return jax.shard_map(
        body, mesh=mesh, in_specs=placed, out_specs=P(None, "prow", None, None), check_vma=False
    )
```

```python
import functools

import jax
import jax.numpy as jnp
from jax import lax
from jax.experimental import pallas as pl
from jax.experimental.pallas import tpu as pltpu
from jax.sharding import PartitionSpec as P

MESH = pl.DeviceIdType.MESH
F32 = jnp.float32
BF16 = jnp.bfloat16
HALVES = 2
SUM_TYPE = BF16


def mm(a, b):
    return jnp.dot(a, b, preferred_element_type=F32)


def mm_t(a, b):
    return lax.dot_general(a, b, (((1,), (1,)), ((), ())), preferred_element_type=F32)


def kernel(
    n_rows, n_cols, n_group,
    rhs_hbm, low_hbm, upp_hbm, linv_hbm, uinv_hbm, pat_hbm,
    out_hbm,
    rhs, low, upp, linv, uinv, pat, low_t, upp_t,
    first, base1, base2, base0, base3, carry, prod, land, slices, fetched, n_hi, n_lo,
    load_sem, pat_sem, cast_send, cast_recv, sum_send, sum_recv, out_send, out_recv,
):
    size = rhs.shape[1]
    width = rhs.shape[2]
    part = width // n_cols
    n_chips = n_cols // HALVES
    half_rows = width // HALVES
    row = lax.axis_index("prow")
    col = lax.axis_index("pcol")
    core = lax.rem(col, HALVES)
    chip = col // HALVES
    owner_col = row // n_group
    place = row % n_group
    n_outer = n_rows // n_group
    is_own = owner_col == col

    barrier = pltpu.get_barrier_semaphore()
    for q in range(n_cols):
        for b in range(n_group):
            src_row = col * n_group + b

            @pl.when(jnp.logical_or(src_row != row, q != col))
            def _():
                pl.semaphore_signal(barrier, inc=1, device_id=(src_row, q), device_id_type=MESH)

        @pl.when(q != col)
        def _():
            pl.semaphore_signal(barrier, inc=1, device_id=(row, q), device_id_type=MESH)

    loads = [
        pltpu.make_async_copy(linv_hbm.at[:, 0], linv, load_sem.at[0]),
        pltpu.make_async_copy(rhs_hbm.at[:, 0], rhs, load_sem.at[1]),
        pltpu.make_async_copy(pat_hbm, pat, pat_sem),
        pltpu.make_async_copy(low_hbm.at[0, 0], low.at[0], load_sem.at[2]),
        pltpu.make_async_copy(uinv_hbm.at[:, 0], uinv, load_sem.at[3]),
        pltpu.make_async_copy(low_hbm.at[1, 0], low.at[1], load_sem.at[4]),
        pltpu.make_async_copy(low_hbm.at[2, 0], low.at[2], load_sem.at[5]),
        pltpu.make_async_copy(upp_hbm.at[:, 0], upp, load_sem.at[6]),
    ]
    for copy in loads:
        copy.start()

    own = pl.ds(pl.multiple_of(core * half_rows + chip * part, part), part)
    in_half = pl.ds(pl.multiple_of(chip * part, part), part)

    def target_row(step):
        i, j = step // n_group, step % n_group
        d_outer = n_outer // 2 + ((i + 1) // 2) * (1 - 2 * (i % 2))
        d_inner = n_group // 2 + ((j + 1) // 2) * (1 - 2 * (j % 2))
        outer = (row // n_group + d_outer) % n_outer
        inner = (row % n_group + d_inner) % n_group
        return outer * n_group + inner

    def cast_ends(rnd):
        source = first.at[own] if rnd == 0 else slices.at[rnd]
        return source, fetched.at[rnd, core, place, in_half]

    def cast_copy(rnd, step):
        source, target = cast_ends(rnd)
        return pltpu.make_async_remote_copy(
            src_ref=source,
            dst_ref=target,
            send_sem=cast_send.at[rnd],
            recv_sem=cast_recv.at[rnd, core],
            device_id=(target_row(step), owner_col),
            device_id_type=MESH,
        )

    def cast_start(rnd):
        def one(step, unused):
            cast_copy(rnd, step).start()
            return unused

        for step in range(n_rows - 1):
            one(step, 0)

        @pl.when(jnp.logical_not(is_own))
        def _():
            cast_copy(rnd, n_rows - 1).start()

        @pl.when(is_own)
        def _():
            source, target = cast_ends(rnd)
            pltpu.make_async_copy(source, target, cast_recv.at[rnd, core]).start()

    def cast_wait(rnd, half):
        whole = fetched.at[rnd, half]
        pltpu.make_async_copy(whole, whole, cast_recv.at[rnd, half]).wait()

    def cast_drain(rnd):
        def one(step, unused):
            cast_copy(rnd, step).wait_send()
            return unused

        lax.fori_loop(0, n_rows - 1, one, 0)

        @pl.when(jnp.logical_not(is_own))
        def _():
            cast_copy(rnd, n_rows - 1).wait_send()

    def sum_copy(rnd, half, other):
        return pltpu.make_async_remote_copy(
            src_ref=prod.at[rnd, half, pl.ds(pl.multiple_of(other * part, part), part)],
            dst_ref=land.at[rnd, col],
            send_sem=sum_send.at[rnd, half],
            recv_sem=sum_recv.at[rnd],
            device_id=(row, other * HALVES + half),
            device_id_type=MESH,
        )

    chip_order = [n_chips // 2] + [d for d in range(1, n_chips) if d != n_chips // 2]

    def scatter(rnd, half, value):
        prod[rnd, half] = value.astype(prod.dtype)
        for step in chip_order:
            sum_copy(rnd, half, lax.rem(chip + step, n_chips)).start()

        @pl.when(core != half)
        def _():
            sum_copy(rnd, half, chip).start()

    def scatter_drain(rnd, half):
        for step in chip_order:
            sum_copy(rnd, half, lax.rem(chip + step, n_chips)).wait_send()

        @pl.when(core != half)
        def _():
            sum_copy(rnd, half, chip).wait_send()

    def summed(rnd, half):
        land[rnd, col] = prod[rnd, half, in_half]
        most = land.at[rnd, pl.ds(0, n_cols - 1)]
        pltpu.make_async_copy(most, most, sum_recv.at[rnd]).wait()
        total = land[rnd, 0].astype(F32)
        for q in range(1, n_cols):
            total = total + land[rnd, q].astype(F32)
        return total

    def out_copy(rnd, level, step):
        return pltpu.make_async_remote_copy(
            src_ref=slices.at[rnd],
            dst_ref=out_hbm.at[level, own],
            send_sem=out_send.at[level],
            recv_sem=out_recv.at[level],
            device_id=(row, lax.rem(col + step, n_cols)),
            device_id_type=MESH,
        )

    peer_order = [4, 3, 5, 2, 6, 1, 7]

    def share(rnd, level):
        for step in peer_order:
            out_copy(rnd, level, step).start()
        pltpu.make_async_copy(slices.at[rnd], out_hbm.at[level, own], out_recv.at[level]).start()

    def share_wait(rnd, level):
        whole = out_hbm.at[level]
        pltpu.make_async_copy(whole, whole, out_recv.at[level]).wait()
        for step in peer_order:
            out_copy(rnd, level, step).wait_send()

    def fold_lower(pair, products):
        for b in range(n_group):
            cols = slice(b * size, (b + 1) * size)
            keep = pat[pair, row, col * n_group + b].astype(F32)
            low_t[pair, cols] = (products(low[pair, :, cols]) * keep).T.astype(BF16)

    def fold_upper(pair, level):
        for b in range(n_group):
            cols = slice(b * size, (b + 1) * size)
            keep = pat[pair, col * n_group + b, row].astype(F32)
            upp_t[pair, cols] = (mm(uinv[level], upp[pair, :, cols]) * keep).T.astype(BF16)

    loads[0].wait()
    loads[1].wait()
    first[...] = mm(linv[0], rhs[0]).T.astype(BF16)

    pl.semaphore_wait(barrier, n_rows + n_cols - 1 - is_own.astype(jnp.int32))

    @pl.when(core == 0)
    def _():
        cast_start(0)

    loads[2].wait()
    loads[3].wait()
    fold_lower(0, lambda block: mm(linv[1], block))
    base1[...] = mm(linv[1], rhs[1]).T
    loads[4].wait()
    both = mm(uinv[2], linv[2])
    n_hi[...] = both.astype(BF16)
    n_lo[...] = (both - n_hi[...].astype(F32)).astype(BF16)

    def through(block):
        return mm(n_hi[...], block) + mm(n_lo[...], block)

    base2[...] = through(rhs[2]).T
    base0[...] = mm_t(first[...], uinv[0])

    loads[5].wait()
    fold_lower(1, through)
    loads[6].wait()
    fold_lower(2, through)
    loads[7].wait()
    fold_upper(2, 1)
    fold_upper(1, 0)
    fold_upper(0, 0)

    @pl.when(core == 1)
    def _():
        cast_start(0)

    for rnd in range(4):
        for half in range(HALVES):
            cast_wait(rnd, half)
            got = jnp.concatenate([fetched[rnd, half, b] for b in range(n_group)], axis=1)
            if rnd == 0:
                value = mm(got, low_t[0])
            elif rnd == 1:
                value = mm(got, low_t[2]) + carry[half]
            elif rnd == 2:
                value = mm(got, upp_t[2])
            else:
                value = mm(got, upp_t[0]) + carry[half]
            scatter(rnd, half, value)
            if rnd == 0:
                carry[half] = mm(got, low_t[1])
            if rnd == 2:
                carry[half] = mm(got, upp_t[1])

            @pl.when(core == half)
            def _():
                base = (lambda: base1[own], lambda: base2[own], lambda: base3[...], lambda: base0[own])[rnd]()
                slices[rnd + 1] = (base - summed(rnd, half)).astype(BF16)
                if rnd < 3:
                    cast_start(rnd + 1)
                if rnd == 0:
                    base3[...] = mm_t(slices[1], uinv[1])
                else:
                    share(rnd + 1, 3 - rnd)

    for rnd in range(4):
        cast_drain(rnd)
        for half in range(HALVES):
            scatter_drain(rnd, half)
    for rnd in range(1, 4):
        share_wait(rnd + 1, 3 - rnd)


def solution(mesh):
    n_rows, n_cols = mesh.shape["prow"], mesh.shape["pcol"]

    def body(right_side, lower_blocks, upper_blocks, lower_inverse, upper_inverse, pattern):
        levels, _, size, width = right_side.shape
        pairs, _, _, span = lower_blocks.shape
        n_group = span // size
        part = width // n_cols
        half_rows = width // HALVES
        any_spec = pl.BlockSpec(memory_space=pl.ANY)
        turned = pl.pallas_call(
            functools.partial(kernel, n_rows, n_cols, n_group),
            out_shape=jax.ShapeDtypeStruct((levels, width, size), BF16),
            in_specs=[any_spec] * 6,
            out_specs=any_spec,
            scratch_shapes=[
                pltpu.VMEM((levels, size, width), BF16),
                pltpu.VMEM((pairs, size, span), BF16),
                pltpu.VMEM((pairs, size, span), BF16),
                pltpu.VMEM((levels, size, size), BF16),
                pltpu.VMEM((levels, size, size), BF16),
                pltpu.SMEM(pattern.shape, jnp.int32),
                pltpu.VMEM((pairs, span, size), BF16),
                pltpu.VMEM((pairs, span, size), BF16),
                pltpu.VMEM((width, size), BF16),
                pltpu.VMEM((width, size), F32),
                pltpu.VMEM((width, size), F32),
                pltpu.VMEM((width, size), F32),
                pltpu.VMEM((part, size), F32),
                pltpu.VMEM((HALVES, half_rows, size), F32),
                pltpu.VMEM((4, HALVES, half_rows, size), SUM_TYPE),
                pltpu.VMEM((4, n_cols, part, size), SUM_TYPE),
                pltpu.VMEM((5, part, size), BF16),
                pltpu.VMEM((4, HALVES, n_group, half_rows, size), BF16),
                pltpu.VMEM((size, size), BF16),
                pltpu.VMEM((size, size), BF16),
                pltpu.SemaphoreType.DMA((7,)),
                pltpu.SemaphoreType.DMA(()),
                pltpu.SemaphoreType.DMA((4,)),
                pltpu.SemaphoreType.DMA((4, HALVES)),
                pltpu.SemaphoreType.DMA((4, HALVES)),
                pltpu.SemaphoreType.DMA((4,)),
                pltpu.SemaphoreType.DMA((3,)),
                pltpu.SemaphoreType.DMA((3,)),
            ],
            compiler_params=pltpu.CompilerParams(collective_id=0, has_side_effects=True, vmem_limit_bytes=24 * 1024 * 1024),
        )(*[pltpu.with_memory_space_constraint(x, pltpu.HBM) for x in (right_side, lower_blocks, upper_blocks, lower_inverse, upper_inverse, pattern)])
        return jnp.swapaxes(turned, 1, 2)[:, None]

    placed = (
        P(None, "prow", None, None),
        P(None, "prow", None, "pcol"),
        P(None, "prow", None, "pcol"),
        P(None, "prow", None, None),
        P(None, "prow", None, None),
        P(),
    )
    return jax.shard_map(
        body, mesh=mesh, in_specs=placed, out_specs=P(None, "prow", None, None), check_vma=False
    )
```

```python
import functools

import jax
import jax.numpy as jnp
from jax import lax
from jax.experimental import pallas as pl
from jax.experimental.pallas import tpu as pltpu
from jax.sharding import PartitionSpec as P

MESH = pl.DeviceIdType.MESH
F32 = jnp.float32
BF16 = jnp.bfloat16
HALVES = 2
SUM_TYPE = BF16


def mm(a, b):
    return jnp.dot(a, b, preferred_element_type=F32)


def mm_t(a, b):
    return lax.dot_general(a, b, (((1,), (1,)), ((), ())), preferred_element_type=F32)


def kernel(
    n_rows, n_cols, n_group,
    rhs_hbm, low_hbm, upp_hbm, linv_hbm, uinv_hbm, pat_hbm,
    out_hbm,
    rhs, low, upp, linv, uinv, pat, low_t, upp_t,
    first, base1, base2, base0, base3, carry, prod, land, slices, fetched, n_hi, n_lo,
    load_sem, pat_sem, cast_send, cast_recv, sum_send, sum_recv, out_send, out_recv,
):
    size = rhs.shape[1]
    width = rhs.shape[2]
    part = width // n_cols
    n_chips = n_cols // HALVES
    half_rows = width // HALVES
    row = lax.axis_index("prow")
    col = lax.axis_index("pcol")
    core = lax.rem(col, HALVES)
    chip = col // HALVES
    owner_col = row // n_group
    place = row % n_group
    n_outer = n_rows // n_group
    is_own = owner_col == col

    barrier = pltpu.get_barrier_semaphore()
    for q in range(n_cols):
        for b in range(n_group):
            src_row = col * n_group + b

            @pl.when(jnp.logical_or(src_row != row, q != col))
            def _():
                pl.semaphore_signal(barrier, inc=1, device_id=(src_row, q), device_id_type=MESH)

        @pl.when(q != col)
        def _():
            pl.semaphore_signal(barrier, inc=1, device_id=(row, q), device_id_type=MESH)

    loads = [
        pltpu.make_async_copy(linv_hbm.at[:, 0], linv, load_sem.at[0]),
        pltpu.make_async_copy(rhs_hbm.at[:, 0], rhs, load_sem.at[1]),
        pltpu.make_async_copy(pat_hbm, pat, pat_sem),
        pltpu.make_async_copy(low_hbm.at[0, 0], low.at[0], load_sem.at[2]),
        pltpu.make_async_copy(uinv_hbm.at[:, 0], uinv, load_sem.at[3]),
        pltpu.make_async_copy(low_hbm.at[1, 0], low.at[1], load_sem.at[4]),
        pltpu.make_async_copy(low_hbm.at[2, 0], low.at[2], load_sem.at[5]),
        pltpu.make_async_copy(upp_hbm.at[:, 0], upp, load_sem.at[6]),
    ]
    for copy in loads:
        copy.start()

    own = pl.ds(pl.multiple_of(core * half_rows + chip * part, part), part)
    in_half = pl.ds(pl.multiple_of(chip * part, part), part)

    def target_row(step):
        i, j = step // n_group, step % n_group
        d_outer = n_outer // 2 + ((i + 1) // 2) * (1 - 2 * (i % 2))
        d_inner = n_group // 2 + ((j + 1) // 2) * (1 - 2 * (j % 2))
        outer = (row // n_group + d_outer) % n_outer
        inner = (row % n_group + d_inner) % n_group
        return outer * n_group + inner

    def cast_ends(rnd):
        source = first.at[own] if rnd == 0 else slices.at[rnd]
        return source, fetched.at[rnd, core, place, in_half]

    def cast_copy(rnd, step):
        source, target = cast_ends(rnd)
        return pltpu.make_async_remote_copy(
            src_ref=source,
            dst_ref=target,
            send_sem=cast_send.at[rnd],
            recv_sem=cast_recv.at[rnd, core],
            device_id=(target_row(step), owner_col),
            device_id_type=MESH,
        )

    def cast_start(rnd):
        def one(step, unused):
            cast_copy(rnd, step).start()
            return unused

        for step in range(n_rows - 1):
            one(step, 0)

        @pl.when(jnp.logical_not(is_own))
        def _():
            cast_copy(rnd, n_rows - 1).start()

        @pl.when(is_own)
        def _():
            source, target = cast_ends(rnd)
            pltpu.make_async_copy(source, target, cast_recv.at[rnd, core]).start()

    def cast_wait(rnd, half):
        whole = fetched.at[rnd, half]
        pltpu.make_async_copy(whole, whole, cast_recv.at[rnd, half]).wait()

    def cast_drain(rnd):
        def one(step, unused):
            cast_copy(rnd, step).wait_send()
            return unused

        lax.fori_loop(0, n_rows - 1, one, 0)

        @pl.when(jnp.logical_not(is_own))
        def _():
            cast_copy(rnd, n_rows - 1).wait_send()

    def sum_copy(rnd, half, other):
        return pltpu.make_async_remote_copy(
            src_ref=prod.at[rnd, half, pl.ds(pl.multiple_of(other * part, part), part)],
            dst_ref=land.at[rnd, col],
            send_sem=sum_send.at[rnd, half],
            recv_sem=sum_recv.at[rnd],
            device_id=(row, other * HALVES + half),
            device_id_type=MESH,
        )

    chip_order = [n_chips // 2] + [d for d in range(1, n_chips) if d != n_chips // 2]

    def scatter(rnd, half, value):
        prod[rnd, half] = value.astype(prod.dtype)
        for step in chip_order:
            sum_copy(rnd, half, lax.rem(chip + step, n_chips)).start()

        @pl.when(core != half)
        def _():
            sum_copy(rnd, half, chip).start()

    def scatter_drain(rnd, half):
        for step in chip_order:
            sum_copy(rnd, half, lax.rem(chip + step, n_chips)).wait_send()

        @pl.when(core != half)
        def _():
            sum_copy(rnd, half, chip).wait_send()

    def summed(rnd, half):
        land[rnd, col] = prod[rnd, half, in_half]
        most = land.at[rnd, pl.ds(0, n_cols - 1)]
        pltpu.make_async_copy(most, most, sum_recv.at[rnd]).wait()
        total = land[rnd, 0].astype(F32)
        for q in range(1, n_cols):
            total = total + land[rnd, q].astype(F32)
        return total

    def out_copy(rnd, level, step):
        return pltpu.make_async_remote_copy(
            src_ref=slices.at[rnd],
            dst_ref=out_hbm.at[level, own],
            send_sem=out_send.at[level],
            recv_sem=out_recv.at[level],
            device_id=(row, lax.rem(col + step, n_cols)),
            device_id_type=MESH,
        )

    peer_order = [4, 3, 5, 2, 6, 1, 7]

    def share(rnd, level):
        for step in peer_order:
            out_copy(rnd, level, step).start()
        pltpu.make_async_copy(slices.at[rnd], out_hbm.at[level, own], out_recv.at[level]).start()

    def share_wait(rnd, level):
        whole = out_hbm.at[level]
        pltpu.make_async_copy(whole, whole, out_recv.at[level]).wait()
        for step in peer_order:
            out_copy(rnd, level, step).wait_send()

    def fold_lower(pair, products):
        for b in range(n_group):
            cols = slice(b * size, (b + 1) * size)
            keep = pat[pair, row, col * n_group + b].astype(F32)
            low_t[pair, cols] = (products(low[pair, :, cols]) * keep).T.astype(BF16)

    def fold_upper(pair, level):
        for b in range(n_group):
            cols = slice(b * size, (b + 1) * size)
            keep = pat[pair, col * n_group + b, row].astype(F32)
            upp_t[pair, cols] = (mm(uinv[level], upp[pair, :, cols]) * keep).T.astype(BF16)

    loads[0].wait()
    loads[1].wait()
    first[...] = mm(linv[0], rhs[0]).T.astype(BF16)

    pl.semaphore_wait(barrier, n_rows + n_cols - 1 - is_own.astype(jnp.int32))

    @pl.when(core == 0)
    def _():
        cast_start(0)

    loads[2].wait()
    loads[3].wait()
    fold_lower(0, lambda block: mm(linv[1], block))
    base1[...] = mm(linv[1], rhs[1]).T
    loads[4].wait()
    both = mm(uinv[2], linv[2])
    n_hi[...] = both.astype(BF16)
    n_lo[...] = (both - n_hi[...].astype(F32)).astype(BF16)

    def through(block):
        return mm(n_hi[...], block) + mm(n_lo[...], block)

    base2[...] = through(rhs[2]).T
    base0[...] = mm_t(first[...], uinv[0])

    loads[5].wait()
    fold_lower(1, through)
    loads[6].wait()
    fold_lower(2, through)
    loads[7].wait()
    fold_upper(2, 1)
    fold_upper(1, 0)
    fold_upper(0, 0)

    @pl.when(core == 1)
    def _():
        cast_start(0)

    for rnd in range(4):
        for half in range(HALVES):
            cast_wait(rnd, half)
            got = jnp.concatenate([fetched[rnd, half, b] for b in range(n_group)], axis=1)
            if rnd == 0:
                value = mm(got, low_t[0])
            elif rnd == 1:
                value = mm(got, low_t[2]) + carry[half]
            elif rnd == 2:
                value = mm(got, upp_t[2])
            else:
                value = mm(got, upp_t[0]) + carry[half]
            scatter(rnd, half, value)

            @pl.when(core == half)
            def _():
                base = (lambda: base1[own], lambda: base2[own], lambda: base3[...], lambda: base0[own])[rnd]()
                slices[rnd + 1] = (base - summed(rnd, half)).astype(BF16)
                if rnd < 3:
                    cast_start(rnd + 1)
                if rnd == 0:
                    base3[...] = mm_t(slices[1], uinv[1])
                else:
                    share(rnd + 1, 3 - rnd)

            if rnd == 0:
                carry[half] = mm(got, low_t[1])
            if rnd == 2:
                carry[half] = mm(got, upp_t[1])

    for rnd in range(4):
        cast_drain(rnd)
        for half in range(HALVES):
            scatter_drain(rnd, half)
    for rnd in range(1, 4):
        share_wait(rnd + 1, 3 - rnd)


def solution(mesh):
    n_rows, n_cols = mesh.shape["prow"], mesh.shape["pcol"]

    def body(right_side, lower_blocks, upper_blocks, lower_inverse, upper_inverse, pattern):
        levels, _, size, width = right_side.shape
        pairs, _, _, span = lower_blocks.shape
        n_group = span // size
        part = width // n_cols
        half_rows = width // HALVES
        any_spec = pl.BlockSpec(memory_space=pl.ANY)
        turned = pl.pallas_call(
            functools.partial(kernel, n_rows, n_cols, n_group),
            out_shape=jax.ShapeDtypeStruct((levels, width, size), BF16),
            in_specs=[any_spec] * 6,
            out_specs=any_spec,
            scratch_shapes=[
                pltpu.VMEM((levels, size, width), BF16),
                pltpu.VMEM((pairs, size, span), BF16),
                pltpu.VMEM((pairs, size, span), BF16),
                pltpu.VMEM((levels, size, size), BF16),
                pltpu.VMEM((levels, size, size), BF16),
                pltpu.SMEM(pattern.shape, jnp.int32),
                pltpu.VMEM((pairs, span, size), BF16),
                pltpu.VMEM((pairs, span, size), BF16),
                pltpu.VMEM((width, size), BF16),
                pltpu.VMEM((width, size), F32),
                pltpu.VMEM((width, size), F32),
                pltpu.VMEM((width, size), F32),
                pltpu.VMEM((part, size), F32),
                pltpu.VMEM((HALVES, half_rows, size), F32),
                pltpu.VMEM((4, HALVES, half_rows, size), SUM_TYPE),
                pltpu.VMEM((4, n_cols, part, size), SUM_TYPE),
                pltpu.VMEM((5, part, size), BF16),
                pltpu.VMEM((4, HALVES, n_group, half_rows, size), BF16),
                pltpu.VMEM((size, size), BF16),
                pltpu.VMEM((size, size), BF16),
                pltpu.SemaphoreType.DMA((7,)),
                pltpu.SemaphoreType.DMA(()),
                pltpu.SemaphoreType.DMA((4,)),
                pltpu.SemaphoreType.DMA((4, HALVES)),
                pltpu.SemaphoreType.DMA((4, HALVES)),
                pltpu.SemaphoreType.DMA((4,)),
                pltpu.SemaphoreType.DMA((3,)),
                pltpu.SemaphoreType.DMA((3,)),
            ],
            compiler_params=pltpu.CompilerParams(collective_id=0, has_side_effects=True, vmem_limit_bytes=24 * 1024 * 1024),
        )(*[pltpu.with_memory_space_constraint(x, pltpu.HBM) for x in (right_side, lower_blocks, upper_blocks, lower_inverse, upper_inverse, pattern)])
        return jnp.swapaxes(turned, 1, 2)[:, None]

    placed = (
        P(None, "prow", None, None),
        P(None, "prow", None, "pcol"),
        P(None, "prow", None, "pcol"),
        P(None, "prow", None, None),
        P(None, "prow", None, None),
        P(),
    )
    return jax.shard_map(
        body, mesh=mesh, in_specs=placed, out_specs=P(None, "prow", None, None), check_vma=False
    )
```
